256 devices in a mesh: dp: 32 (over y, x, core), seq: 8 (over z).
Axes of the slice: x: 4, y: 4, z: 8, core: 2. Of those that a mesh axis runs over, the one named last changes fastest.
Arguments:
- tokens: bfloat16 [65536, 2048], P(('dp', 'seq')), may hold values from -24 to 24
- queries: bfloat16 [65536, 1024], P(('dp', 'seq')), may hold values from -6 to 6
- kv_weight: bfloat16 [2048, 2048], P('seq'), may hold values from -0.0625 to 0.0625
- out_grad: bfloat16 [65536, 1024], P(('dp', 'seq')), may hold values from -6 to 6
Outputs:
- output: bfloat16 [65536, 1024], P(('dp', 'seq'))
- token_grad: bfloat16 [65536, 2048], P(('dp', 'seq'))
- query_grad: bfloat16 [65536, 1024], P(('dp', 'seq'))
- weight_grad: float32 [2048, 2048], P(('dp', 'seq'))
The draws below stay inside these ranges and needn't reach their ends.
All inputs are finite; a program needn't handle non-finite values.
Results may differ from the reference program's by a relative error of at most 0.014.
Values may be sent and summed in bfloat16 or wider, within the bound.
No kernel may reach another device: no remote copies, remote signals or barrier semaphores. Data moves between devices by JAX's collectives and lax.ppermute only.
A program may use at most 128 MiB of HBM per device.

```python
import math
import jax
import jax.numpy as jnp
from jax import lax

D = 2048
HEADS = 8
HD = 128
TOK_DEV = 256
HW = 1024
LENGTH = 2048
TOKENS = 65536


def draw_kv_weight(key, part):
    first_key = jax.random.fold_in(key, 11)
    second_key = jax.random.fold_in(key, 12)
    columns = 2 * HEADS * HD
    entries = jax.random.truncated_normal(first_key, -4.0, 4.0, (D, columns), jnp.float32)
    column_scale = jnp.exp(jax.random.uniform(second_key, (columns,), jnp.float32, math.log(0.3), math.log(3.0)))
    limit = 0.0625
    values = jnp.clip(entries * column_scale[None, :] * (1.0 / math.sqrt(D)), -limit, limit)
    return values.astype(jnp.bfloat16)


def with_spikes(result, own_key, source, target, blocks, factor):
    def block_of(dim):
        return (jnp.arange(result.shape[dim]) // (result.shape[dim] // blocks)).reshape((-1,) + (1,) * (result.ndim - 1 - dim))

    first = jax.random.permutation(own_key, blocks)[block_of(target)]
    other_side = (block_of(target) + blocks // 2) % blocks
    return jnp.where((block_of(source) == first) | (block_of(source) == other_side), factor * result, result)


def level_of(own_key, dims, cuts, least, largest):
    level, own = 1.0, jax.random.fold_in(own_key, 6)
    for position, shards_of in cuts:
        draws = jnp.exp(jax.random.uniform(jax.random.fold_in(own, position), (shards_of,), jnp.float32, least / len(cuts), largest / len(cuts)))
        level = level * jnp.repeat(draws, dims[position] // shards_of).reshape([-1 if axis == position else 1 for axis in range(len(dims))])
    return level


def bell_draw(key, extent, width, most, pieces=(), dtype=jnp.bfloat16):
    level = level_of(key, extent, pieces, -0.22, 0.18) if pieces else 1.0
    result = jax.random.normal(key, extent, jnp.float32) * width * level
    return jnp.minimum(jnp.maximum(result, -most), most).astype(dtype)


def bell_draw_with(key, extent, scale, reach, pieces, heavy, dtype=jnp.bfloat16):
    values = scale * jax.random.normal(key, extent, jnp.float32)
    if pieces:
        values = values * level_of(key, extent, pieces, -0.22, 0.18)
    return jnp.clip(with_spikes(values, jax.random.fold_in(key, 3), *heavy), -reach, reach).astype(dtype)


def setup_inputs(seed: int = 0) -> dict:
    arg_keys = jax.random.split(jax.random.key(seed), 5)
    tokens = bell_draw_with(arg_keys[0], (TOKENS, D), 1.0, 24.0, ((0, 256),), (0, 1, 256, 6.0))
    queries = bell_draw(arg_keys[1], (TOKENS, HW), 1.0, 6.0, ((0, 256),))
    kv_weight = draw_kv_weight(jax.random.fold_in(arg_keys[4], 71), 0)
    out_grad = bell_draw(arg_keys[3], (TOKENS, HW), 1.0, 6.0, ((0, 256),))
    return {"tokens": tokens, "queries": queries, "kv_weight": kv_weight, "out_grad": out_grad}


epsilon = 1e-05

def feature(inputs):
    return jnp.where(inputs > 0, inputs + 1.0, jnp.exp(jnp.minimum(inputs, 0.0)))

def feature_slope(inputs):
    return jnp.where(inputs > 0, 1.0, jnp.exp(jnp.minimum(inputs, 0.0)))

def contract(formula, first_op, second_op):
    return jnp.einsum(formula, first_op, second_op, precision=lax.Precision.HIGHEST)

def reference(tokens, queries, kv_weight, out_grad):
    head_width = HEADS * HD
    sequences = TOKENS // LENGTH
    blocks = LENGTH // TOK_DEV
    positions = jnp.arange(TOK_DEV)
    causal = (positions[:, None] >= positions[None, :]).astype(jnp.float32)[None]

    def one_sequence(summed, inputs):
        seq_tokens, seq_queries, seq_grad = inputs
        kv_local = jnp.dot(seq_tokens, kv_weight, preferred_element_type=jnp.float32).astype(jnp.bfloat16)
        query_f = seq_queries.astype(jnp.float32)
        key_f = kv_local[:, :head_width].astype(jnp.float32)
        value_f = kv_local[:, head_width:].astype(jnp.float32).reshape(blocks, TOK_DEV, HEADS, HD)
        q_feat = feature(query_f).reshape(blocks, TOK_DEV, HEADS, HD)
        k_feat = feature(key_f).reshape(blocks, TOK_DEV, HEADS, HD)

        def forward(carried, block_in):
            q_block, k_block, v_block = block_in
            scores = contract('thd,shd->hts', q_block, k_block) * causal
            attended = contract('hts,she->the', scores, v_block) + contract('thd,hde->the', q_block, carried)
            return (carried + contract('thd,the->hde', k_block, v_block), (attended, carried))
        zero_state = jnp.zeros((HEADS, HD, HD), jnp.float32)
        _, (attended, before) = lax.scan(forward, zero_state, (q_feat, k_feat, value_f))
        radius = jnp.sqrt(lax.optimization_barrier(jnp.mean(attended * attended, axis=-1, keepdims=True)) + epsilon)
        normed = attended / radius
        output = normed.astype(jnp.bfloat16).reshape(LENGTH, head_width)
        grad_f = seq_grad.astype(jnp.float32).reshape(blocks, TOK_DEV, HEADS, HD)
        grad_att = (grad_f - normed * lax.optimization_barrier(jnp.mean(grad_f * normed, axis=-1, keepdims=True))) / radius

        def backward(carried, block_in):
            q_block, k_block, v_block, g_block, prior = block_in
            scores = contract('thd,shd->hts', q_block, k_block) * causal
            mixed_w = contract('the,she->hts', g_block, v_block) * causal
            grad_qf = contract('hts,shd->thd', mixed_w, k_block) + contract('the,hde->thd', g_block, prior)
            grad_kf = contract('hts,thd->shd', mixed_w, q_block) + contract('she,hde->shd', v_block, carried)
            grad_val = contract('hts,the->she', scores, g_block) + contract('shd,hde->she', k_block, carried)
            return (carried + contract('thd,the->hde', q_block, g_block), (grad_qf, grad_kf, grad_val))
        _, (grad_qf, grad_kf, grad_val) = lax.scan(backward, zero_state, (q_feat, k_feat, value_f, grad_att, before), reverse=True)
        query_grad = (grad_qf.reshape(LENGTH, head_width) * feature_slope(query_f)).astype(jnp.bfloat16)
        key_grad = (grad_kf.reshape(LENGTH, head_width) * feature_slope(key_f)).astype(jnp.bfloat16)
        kv_grad = jnp.concatenate([key_grad, grad_val.reshape(LENGTH, head_width).astype(jnp.bfloat16)], axis=1)
        token_grad = lax.dot_general(kv_grad, kv_weight, (((1,), (1,)), ((), ())), preferred_element_type=jnp.float32).astype(jnp.bfloat16)
        summed = summed + lax.dot_general(seq_tokens, kv_grad, (((0,), (0,)), ((), ())), preferred_element_type=jnp.float32)
        return (summed, (output, token_grad, query_grad))
    grads, (outputs, token_grads, query_grads) = lax.scan(one_sequence, jnp.zeros((D, 2 * head_width), jnp.float32), (tokens.reshape(sequences, LENGTH, D), queries.reshape(sequences, LENGTH, head_width), out_grad.reshape(sequences, LENGTH, head_width)))
    weight_grad = grads * (1.0 / jnp.sqrt(jnp.float32(TOKENS)))
    return (outputs.reshape(TOKENS, head_width), token_grads.reshape(TOKENS, D), query_grads.reshape(TOKENS, head_width), weight_grad)
```

```python
import math

import jax
import jax.numpy as jnp
from jax import lax
from jax.sharding import Mesh
from jax.sharding import PartitionSpec as P

HEADS = 8
HD = 128
EPSILON = 1e-05
BF = jnp.bfloat16
F32 = jnp.float32


def feature(inputs):
    return jnp.where(inputs > 0, inputs + 1.0, jnp.exp(jnp.minimum(inputs, 0.0)))


def feature_slope(inputs):
    return jnp.where(inputs > 0, 1.0, jnp.exp(jnp.minimum(inputs, 0.0)))


def contract(formula, first_op, second_op):
    return jnp.einsum(
        formula, first_op.astype(BF), second_op.astype(BF), preferred_element_type=F32
    )


def swap_cores(x):
    return lax.ppermute(x, "core", [(0, 1), (1, 0)])


def gather_weights(kv_weight):
    rows = kv_weight.shape[0]
    planes = lax.axis_size(("y", "x", "core"))
    part = rows // planes
    mine = lax.dynamic_slice_in_dim(
        kv_weight, lax.axis_index(("y", "x", "core")) * part, part, 0
    )
    along_z = lax.all_gather(mine, "z", axis=0)
    everything = lax.all_gather(along_z, ("y", "x", "core"), axis=0)
    return everything.transpose(1, 0, 2, 3).reshape(-1, kv_weight.shape[1])


def other_shards(state, later):
    everything = lax.all_gather(state.astype(BF), "z")
    place = lax.axis_index("z")
    total = jnp.zeros(state.shape, F32)
    for k in range(lax.axis_size("z")):
        reached = k > place if later else k < place
        total = total + jnp.where(reached, everything[k].astype(F32), 0.0)
    return total.astype(BF)


def on_device(tokens, queries, kv_weight, out_grad):
    local_rows = tokens.shape[0]
    head_width = HEADS * HD
    core = lax.axis_index("core")
    by_core = tokens.reshape(local_rows, -1, 2, 64)
    kept = lax.dynamic_index_in_dim(by_core, core, 2, keepdims=False).reshape(local_rows, -1)
    sent = lax.dynamic_index_in_dim(by_core, 1 - core, 2, keepdims=False).reshape(local_rows, -1)
    chip_tokens = jnp.concatenate([kept, swap_cores(sent)], axis=0)

    weights = gather_weights(kv_weight)
    kv_local = jnp.dot(tokens, weights, preferred_element_type=F32).astype(BF)
    query_f = queries.astype(F32)
    key_f = kv_local[:, :head_width].astype(F32)
    value = kv_local[:, head_width:].reshape(local_rows, HEADS, HD)
    q_feat = feature(query_f).astype(BF).reshape(local_rows, HEADS, HD)
    k_feat = feature(key_f).astype(BF).reshape(local_rows, HEADS, HD)
    positions = jnp.arange(local_rows)
    causal = (positions[:, None] >= positions[None, :])[None]
    before = other_shards(contract("thd,the->hde", k_feat, value), False)
    scores = jnp.where(causal, contract("thd,shd->hts", q_feat, k_feat), 0.0).astype(BF)
    attended = contract("hts,she->the", scores, value) + contract("thd,hde->the", q_feat, before)
    radius = jnp.sqrt(jnp.mean(attended * attended, axis=-1, keepdims=True) + EPSILON)
    normed = attended / radius
    output = normed.astype(BF).reshape(local_rows, head_width)
    grad_f = out_grad.astype(F32).reshape(local_rows, HEADS, HD)
    grad_att = (grad_f - normed * jnp.mean(grad_f * normed, axis=-1, keepdims=True)) / radius
    grad_att = grad_att.astype(BF)
    later_sum = other_shards(contract("thd,the->hde", q_feat, grad_att), True)
    mixed_w = jnp.where(causal, contract("the,she->hts", grad_att, value), 0.0).astype(BF)
    grad_qf = contract("hts,shd->thd", mixed_w, k_feat) + contract("the,hde->thd", grad_att, before)
    grad_kf = contract("hts,thd->shd", mixed_w, q_feat) + contract(
        "she,hde->shd", value, later_sum
    )
    grad_val = contract("hts,the->she", scores, grad_att) + contract(
        "shd,hde->she", k_feat, later_sum
    )
    query_grad = (grad_qf.reshape(local_rows, head_width) * feature_slope(query_f)).astype(BF)
    key_grad = (grad_kf.reshape(local_rows, head_width) * feature_slope(key_f)).astype(BF)
    kv_grad = jnp.concatenate([key_grad, grad_val.reshape(local_rows, head_width).astype(BF)], axis=1)
    chip_grad = jnp.concatenate([kv_grad, swap_cores(kv_grad)], axis=0)
    grad_scale = 1.0 / math.sqrt(local_rows * lax.axis_size(("y", "x", "core", "z")))
    partial = lax.dot_general(
        chip_tokens, chip_grad, (((0,), (0,)), ((), ())), preferred_element_type=F32
    )
    plane = lax.psum_scatter(
        (partial * grad_scale).astype(BF), ("y", "x"), scatter_dimension=0, tiled=True
    )
    weight_grad = lax.psum_scatter(plane.astype(F32), "z", scatter_dimension=0, tiled=True)
    token_grad = lax.dot_general(
        kv_grad, weights, (((1,), (1,)), ((), ())), preferred_element_type=F32
    ).astype(BF)
    return (output, token_grad, query_grad, weight_grad)


def solution(mesh):
    shape = dict(mesh.shape)
    fine = Mesh(mesh.devices.reshape(4, shape["dp"] // 8, 2, shape["seq"]), ("y", "x", "core", "z"))
    rows = P(("y", "x", "core", "z"), None)
    return jax.shard_map(
        on_device,
        mesh=fine,
        in_specs=(rows, rows, P("z", None), rows),
        out_specs=(rows, rows, rows, rows),
        check_vma=False,
    )
```

```python
import math

import jax
import jax.numpy as jnp
from jax import lax
from jax.experimental import pallas as pl
from jax.experimental.pallas import tpu as pltpu
from jax.sharding import Mesh
from jax.sharding import PartitionSpec as P

HD = 128
EPSILON = 1e-05
BF = jnp.bfloat16
F32 = jnp.float32
VMEM = pl.BlockSpec(memory_space=pltpu.VMEM)
ANY = pl.BlockSpec(memory_space=pl.ANY)


def feature(u):
    return jnp.where(u > 0, u + 1.0, jnp.exp(jnp.minimum(u, 0.0)))


def slope(u):
    return jnp.where(u > 0, 1.0, jnp.exp(jnp.minimum(u, 0.0)))


def dot(a, b, da, db):
    return lax.dot_general(a, b, (((da,), (db,)), ((), ())), preferred_element_type=F32)


def call(body, outs, *args, in_specs=None, scratch=(), flops=0):
    size = sum(math.prod(a.shape) * a.dtype.itemsize for a in args)
    size += sum(math.prod(s) * jnp.dtype(d).itemsize for s, d in outs)
    return pl.pallas_call(
        body,
        out_shape=[jax.ShapeDtypeStruct(s, d) for s, d in outs],
        in_specs=in_specs or [VMEM] * len(args),
        out_specs=[VMEM] * len(outs),
        scratch_shapes=list(scratch),
        cost_estimate=pl.CostEstimate(flops=flops, bytes_accessed=size, transcendentals=0),
    )(*args)


def shift(x, axis, step):
    size = lax.axis_size(axis)
    return lax.ppermute(x, axis, [(i, (i + step) % size) for i in range(size)])


def key_value_kernel(own, sib, *refs):
    pieces, (w_ref, kv_own, kv_sib, state), sems = refs[:8], refs[8:12], refs[12]
    y, x = lax.axis_index("y"), lax.axis_index("x")
    copies = []
    for half in range(2):
        for e in range(4):
            for d in range(4):
                py, px = (y - e, x - d) if half == 0 else (y - d, x - e)
                place = lax.rem(py + 4, 4) * 4 + lax.rem(px + 4, 4)
                copies.append(
                    pltpu.make_async_copy(
                        pieces[half * 4 + e].at[d],
                        w_ref.at[:, place, :, pl.ds(half * 512, 512)],
                        sems.at[len(copies)],
                    )
                )
    for c in copies:
        c.start()
    for c in copies:
        c.wait()

    def tile(n, _):
        at = pl.ds(pl.multiple_of(n * 256, 256), 256)
        w = w_ref[:, :, :, at].reshape(2048, 256)
        kv_own[:, at] = dot(own[...], w, 1, 0).astype(BF)
        kv_sib[:, at] = dot(sib[...], w, 1, 0).astype(BF)
        return 0

    lax.fori_loop(0, 4, tile, 0)
    for s, kv in enumerate((kv_own, kv_sib)):
        for h in range(4):
            k = feature(kv[:, h * HD : (h + 1) * HD].astype(F32)).astype(BF)
            v = kv[:, 512 + h * HD : 512 + (h + 1) * HD]
            state[s * 4 + h] = dot(k, v, 0, 0).astype(BF)


def sums_kernel(later, states, out):
    order = list(range(states.shape[0]))
    if later:
        order.reverse()
    total = jnp.zeros(states.shape[1:], F32)
    for k in order:
        out[k] = total.astype(BF)
        total = total + states[k].astype(F32)


def causal():
    shape = (256, 256)
    return lax.broadcasted_iota(jnp.int32, shape, 0) >= lax.broadcasted_iota(jnp.int32, shape, 1)


def own_heads(ref, h):
    at = lax.axis_index("core") * 512 + h * HD
    return ref[:, pl.ds(pl.multiple_of(at, HD), HD)].astype(F32)


def forward_kernel(
    q_own, q_sib, g_own, g_sib, kv_own, kv_sib, before, o_own, o_sib, a_own, a_sib, state
):
    mask = causal()
    rows = ((q_own, g_own, kv_own, o_own, a_own), (q_sib, g_sib, kv_sib, o_sib, a_sib))
    for s, (q_ref, g_ref, kv, o_ref, a_ref) in enumerate(rows):
        for h in range(4):
            at = slice(h * HD, (h + 1) * HD)
            if s == 0:
                q, g = own_heads(q_ref, h), own_heads(g_ref, h)
            else:
                q, g = q_ref[:, at].astype(F32), g_ref[:, at].astype(F32)
            q = feature(q).astype(BF)
            k = feature(kv[:, at].astype(F32)).astype(BF)
            v = kv[:, 512 + h * HD : 512 + (h + 1) * HD]
            scores = jnp.where(mask, dot(q, k, 1, 1), 0.0).astype(BF)
            attended = dot(scores, v, 1, 0) + dot(q, before[s * 4 + h], 1, 0)
            power = jnp.mean(attended * attended, axis=-1, keepdims=True) + EPSILON
            inverse = 1.0 / jnp.sqrt(power)
            normed = attended * inverse
            along = jnp.mean(g * normed, axis=-1, keepdims=True)
            grad = ((g - normed * along) * inverse).astype(BF)
            o_ref[:, at] = normed.astype(BF)
            a_ref[:, at] = grad
            state[s * 4 + h] = dot(q, grad, 0, 0).astype(BF)


def backward_kernel(
    q_own, q_sib, kv_own, kv_sib, a_own, a_sib, before, after, dq_own, dq_sib, dkv_own, dkv_sib
):
    mask = causal()
    rows = ((q_own, kv_own, a_own, dq_own, dkv_own), (q_sib, kv_sib, a_sib, dq_sib, dkv_sib))
    for s, (q_ref, kv, a_ref, dq, dkv) in enumerate(rows):
        for h in range(4):
            at = slice(h * HD, (h + 1) * HD)
            vat = slice(512 + h * HD, 512 + (h + 1) * HD)
            qu = own_heads(q_ref, h) if s == 0 else q_ref[:, at].astype(F32)
            ku = kv[:, at].astype(F32)
            q, k, v, a = feature(qu).astype(BF), feature(ku).astype(BF), kv[:, vat], a_ref[:, at]
            prior, rest = before[s * 4 + h], after[s * 4 + h]
            scores = jnp.where(mask, dot(q, k, 1, 1), 0.0).astype(BF)
            mixed = jnp.where(mask, dot(a, v, 1, 1), 0.0).astype(BF)
            grad_q = dot(mixed, k, 1, 0) + dot(a, prior, 1, 1)
            grad_k = dot(mixed, q, 0, 0) + dot(v, rest, 1, 1)
            grad_v = dot(scores, a, 0, 0) + dot(k, rest, 1, 0)
            dq[:, at] = (grad_q * slope(qu)).astype(BF)
            dkv[:, at] = (grad_k * slope(ku)).astype(BF)
            dkv[:, vat] = grad_v.astype(BF)


def partial_kernel(tok_own, tok_sib, dkv_own, dkv_sib, *outs):
    y, x = lax.axis_index("y"), lax.axis_index("x")
    for dy in range(4):
        for dx in range(4):
            ty, tx = lax.rem(y + dy, 4), lax.rem(x + dx, 4)
            at = pl.ds(pl.multiple_of((ty * 4 + tx) * HD, HD), HD)
            part = dot(tok_own[:, at], dkv_own[...], 0, 0) + dot(tok_sib[:, at], dkv_sib[...], 0, 0)
            a_ref, b_ref = outs[dx], outs[4 + dy]
            a_ref[ty] = part[:, :512].astype(a_ref.dtype)
            b_ref[tx] = part[:, 512:].astype(b_ref.dtype)


def plane_kernel(*refs):
    for half, axis in ((0, "y"), (1, "x")):
        ins, outs = refs[half * 4 : half * 4 + 4], refs[8 + half * 4 : 12 + half * 4]
        here = lax.axis_index(axis)
        for e in range(4):
            at = lax.rem(here + e, 4)
            total = ins[0][at]
            for r in ins[1:]:
                total = total + r[at].astype(F32)
            outs[e][...] = total.astype(outs[e].dtype)


def column_kernel(*refs):
    out = refs[8]
    for half in range(2):
        total = refs[half * 4][...]
        for r in refs[half * 4 + 1 : half * 4 + 4]:
            total = total + r[...].astype(F32)
        out[:, :, half * 512 : half * 512 + 512] = total.reshape(16, 8, 512).astype(BF)


def last_kernel(scale, parts, out):
    for c in range(2):
        total = parts[c * 8].astype(F32)
        for k in range(1, 8):
            total = total + parts[c * 8 + k].astype(F32)
        total = total * scale
        for half in range(2):
            at = half * 1024 + c * 512
            out[:, at : at + 512] = total[:, half * 512 : half * 512 + 512]


def token_kernel(dkv_a, dkv_b, w_a, w_b, out):
    def tile(n, _):
        wa = w_a[n].reshape(256, 1024)
        wb = w_b[n].reshape(256, 1024)
        at = pl.ds(pl.multiple_of(n * 256, 256), 256)
        out[:, at] = (dot(dkv_a[...], wa, 1, 1) + dot(dkv_b[...], wb, 1, 1)).astype(BF)
        return 0

    lax.fori_loop(0, 8, tile, 0)


def on_device(tokens, queries, kv_weight, out_grad):
    rows = tokens.shape[0]
    core = lax.axis_index("core")

    def swap(x):
        return lax.ppermute(x, "core", [(0, 1), (1, 0)])

    def theirs(x):
        return swap(lax.dynamic_slice_in_dim(x, (1 - core) * 512, 512, 1))

    place = lax.axis_index(("y", "x"))
    mine = lax.dynamic_slice_in_dim(kv_weight, place * 16, 16, 0).reshape(16, 2, 2, 512)
    mine = lax.dynamic_index_in_dim(mine, core, 2, keepdims=False).reshape(16, 1024)
    along_z = lax.all_to_all(jnp.broadcast_to(mine[None], (8, 16, 1024)), "z", 0, 0, tiled=True)
    a0, b0 = along_z[:, :, :512], along_z[:, :, 512:]
    first = [(shift(a0, "x", d), shift(b0, "y", d)) for d in (2, 1, 3)]
    (a2, b2), (a1, b1), (a3, b3) = first
    a = jnp.stack([a0, a1, a2, a3])
    b = jnp.stack([b0, b1, b2, b3])
    (p2, r2), (p1, r1), (p3, r3) = [(shift(a, "y", e), shift(b, "x", e)) for e in (2, 1, 3)]

    sib_tokens = swap(tokens)
    sib_q, sib_g = theirs(queries), theirs(out_grad)
    half = ((rows, 512), BF)
    whole = ((rows, 1024), BF)
    states = ((8, HD, HD), BF)
    w, kv_own, kv_sib, state = call(
        key_value_kernel,
        [((8, 16, 16, 1024), BF), whole, whole, states],
        tokens, sib_tokens, a, p1, p2, p3, b, r1, r2, r3,
        in_specs=[VMEM] * 2 + [ANY] * 8,
        scratch=[pltpu.SemaphoreType.DMA((32,))],
        flops=2 * 512 * 2048 * 1024,
    )
    sib_w = swap(w)

    def exchange(x, later):
        x = lax.all_to_all(x, "z", 0, 0, tiled=True)
        (x,) = call(lambda i, o: sums_kernel(later, i, o), [states], x)
        return lax.all_to_all(x, "z", 0, 0, tiled=True)

    before = exchange(state, False)
    o_own, o_sib, a_own, a_sib, state = call(
        forward_kernel,
        [half, half, half, half, states],
        queries, sib_q, out_grad, sib_g, kv_own, kv_sib, before,
        flops=2 * 8 * 256 * 128 * 768,
    )
    after = exchange(state, True)
    dq_own, dq_sib, dkv_own, dkv_sib = call(
        backward_kernel,
        [half, half, whole, whole],
        queries, sib_q, kv_own, kv_sib, a_own, a_sib, before, after,
        flops=2 * 8 * 256 * 128 * 1664,
    )

    full = ((4, 128, 512), F32)
    sent = ((4, 128, 512), BF)
    parts = call(
        partial_kernel,
        [full, sent, sent, sent, full, sent, sent, sent],
        tokens, sib_tokens, dkv_own, dkv_sib,
        flops=2 * 512 * 2048 * 1024,
    )
    wa, wb = {}, {}
    for d in (2, 1, 3):
        wa[d], wb[d] = shift(parts[d], "x", d), shift(parts[4 + d], "y", d)
    full = ((128, 512), F32)
    sent = ((128, 512), BF)
    parts = call(
        plane_kernel,
        [full, sent, sent, sent, full, sent, sent, sent],
        parts[0], wa[1], wa[2], wa[3], parts[4], wb[1], wb[2], wb[3],
    )
    wa, wb = {}, {}
    for d in (2, 1, 3):
        wa[d], wb[d] = shift(parts[d], "y", d), shift(parts[4 + d], "x", d)
    (column,) = call(
        column_kernel,
        [((16, 8, 1024), BF)],
        parts[0], wa[1], wa[2], wa[3], parts[4], wb[1], wb[2], wb[3],
    )
    column = lax.all_to_all(column, ("core", "z"), 0, 0, tiled=True)
    scale = 1.0 / math.sqrt(rows * lax.axis_size(("y", "x", "core", "z")))
    (weight_grad,) = call(lambda i, o: last_kernel(scale, i, o), [((8, 2048), F32)], column)

    dkv_rest = swap(dkv_sib)
    (token_grad,) = call(
        token_kernel, [((rows, 2048), BF)], dkv_own, dkv_rest, w, sib_w, flops=2 * 256 * 2048 * 2048
    )

    def joined(x, sib):
        sib = swap(sib)
        zero = core == 0
        return jnp.concatenate([jnp.where(zero, x, sib), jnp.where(zero, sib, x)], axis=1)

    return (joined(o_own, o_sib), token_grad, joined(dq_own, dq_sib), weight_grad)


def solution(mesh):
    fine = Mesh(mesh.devices.reshape(4, 4, 2, 8), ("y", "x", "core", "z"))
    rows = P(("y", "x", "core", "z"), None)
    return jax.shard_map(
        on_device,
        mesh=fine,
        in_specs=(rows, rows, P("z", None), rows),
        out_specs=(rows, rows, rows, rows),
        check_vma=False,
    )
```

```python
import functools
import math

import jax
import jax.numpy as jnp
from jax import lax
from jax.experimental import pallas as pl
from jax.experimental.pallas import tpu as pltpu
from jax.sharding import Mesh
from jax.sharding import PartitionSpec as P

HD = 128
EPSILON = 1e-05
BF = jnp.bfloat16
F32 = jnp.float32
VMEM = pl.BlockSpec(memory_space=pltpu.VMEM)
ANY = pl.BlockSpec(memory_space=pl.ANY)


def feature(u):
    return jnp.where(u > 0, u + 1.0, jnp.exp(jnp.minimum(u, 0.0)))


def slope(u):
    return jnp.where(u > 0, 1.0, jnp.exp(jnp.minimum(u, 0.0)))


def dot(a, b, da, db):
    return lax.dot_general(a, b, (((da,), (db,)), ((), ())), preferred_element_type=F32)


def call(body, outs, *args, in_specs=None, scratch=(), flops=0):
    size = sum(math.prod(a.shape) * a.dtype.itemsize for a in args)
    size += sum(math.prod(s) * jnp.dtype(d).itemsize for s, d in outs)
    return pl.pallas_call(
        body,
        out_shape=[jax.ShapeDtypeStruct(s, d) for s, d in outs],
        in_specs=in_specs or [VMEM] * len(args),
        out_specs=[VMEM] * len(outs),
        scratch_shapes=list(scratch),
        cost_estimate=pl.CostEstimate(flops=flops, bytes_accessed=size, transcendentals=0),
    )(*args)


def shift(x, axis, step):
    size = lax.axis_size(axis)
    return lax.ppermute(x, axis, [(i, (i + step) % size) for i in range(size)])


def key_value_kernel(own, sib, *refs):
    pieces, (w_ref, kv_own, kv_sib, state), sems = refs[:8], refs[-5:-1], refs[-1]
    y, x = lax.axis_index("y"), lax.axis_index("x")
    copies = []
    for half in range(2):
        for e in range(4):
            for d in range(4):
                py, px = (y - e, x - d) if half == 0 else (y - d, x - e)
                place = lax.rem(py + 4, 4) * 4 + lax.rem(px + 4, 4)
                copies.append(
                    pltpu.make_async_copy(
                        pieces[half * 4 + e].at[d],
                        w_ref.at[:, place, :, pl.ds(half * 256, 256)],
                        sems.at[len(copies)],
                    )
                )
    for c in copies:
        c.start()
    for c in copies:
        c.wait()

    def tile(n, _):
        at = pl.ds(pl.multiple_of(n * 256, 256), 256)
        w = w_ref[:, :, :, at].reshape(2048, 256)
        kv_own[:, at] = dot(own[...], w, 1, 0).astype(BF)
        kv_sib[:, at] = dot(sib[...], w, 1, 0).astype(BF)
        return 0

    lax.fori_loop(0, 2, tile, 0)
    for s, kv in enumerate((kv_own, kv_sib)):
        for h in range(2):
            k = feature(kv[:, h * HD : (h + 1) * HD].astype(F32)).astype(BF)
            v = kv[:, 256 + h * HD : 256 + (h + 1) * HD]
            state[s * 2 + h] = dot(k, v, 0, 0).astype(BF)


def sums_kernel(later, states, out):
    order = list(range(states.shape[0]))
    if later:
        order.reverse()
    total = jnp.zeros(states.shape[1:], F32)
    for k in order:
        out[k] = total.astype(BF)
        total = total + states[k].astype(F32)


def causal():
    shape = (256, 256)
    return lax.broadcasted_iota(jnp.int32, shape, 0) >= lax.broadcasted_iota(jnp.int32, shape, 1)


def head(h, start=0):
    return pl.ds(pl.multiple_of(start + h * HD, HD), HD)


def own_heads(ref, group, h):
    return ref[:, head(h, lax.axis_index("core") * 512 + group * 256)].astype(F32)


def sib_heads(ref, group, h):
    return ref[:, head(h, group * 256)].astype(F32)


def forward_kernel(group, q_own, q_sib, g_own, g_sib, kv_own, kv_sib, before, *refs):
    o_own, o_sib, a_own, a_sib, state = refs[-5:]
    mask = causal()
    rows = (
        (own_heads, q_own, g_own, kv_own, o_own, a_own),
        (sib_heads, q_sib, g_sib, kv_sib, o_sib, a_sib),
    )
    for s, (heads, q_ref, g_ref, kv, o_ref, a_ref) in enumerate(rows):

        def step(h, _):
            at = head(h)
            q, g = heads(q_ref, group, h), heads(g_ref, group, h)
            q = feature(q).astype(BF)
            k = feature(kv[:, at].astype(F32)).astype(BF)
            v = kv[:, head(h, 256)]
            scores = jnp.where(mask, dot(q, k, 1, 1), 0.0).astype(BF)
            attended = dot(scores, v, 1, 0) + dot(q, before[s * 2 + h], 1, 0)
            power = jnp.mean(attended * attended, axis=-1, keepdims=True) + EPSILON
            inverse = lax.rsqrt(power)
            normed = attended * inverse
            along = jnp.mean(g * normed, axis=-1, keepdims=True)
            grad = ((g - normed * along) * inverse).astype(BF)
            o_ref[:, at] = normed.astype(BF)
            a_ref[:, at] = grad
            state[s * 2 + h] = dot(q, grad, 0, 0).astype(BF)
            return 0

        lax.fori_loop(0, 2, step, 0)


def backward_kernel(
    group, q_own, q_sib, kv_own, kv_sib, a_own, a_sib, o_sib, before, after, *refs
):
    dq_own, dkv_own, back = refs[-3:]
    mask = causal()
    back[:, 768:] = o_sib[...]
    rows = (
        (own_heads, q_own, kv_own, a_own, dq_own, 0, dkv_own),
        (sib_heads, q_sib, kv_sib, a_sib, back, 512, back),
    )
    for s, (heads, q_ref, kv, a_ref, dq, dq_at, dkv) in enumerate(rows):

        def step(h, _):
            at, vat = head(h), head(h, 256)
            qu = heads(q_ref, group, h)
            ku = kv[:, at].astype(F32)
            q, k, v, a = feature(qu).astype(BF), feature(ku).astype(BF), kv[:, vat], a_ref[:, at]
            prior, rest = before[s * 2 + h], after[s * 2 + h]
            scores = jnp.where(mask, dot(q, k, 1, 1), 0.0).astype(BF)
            mixed = jnp.where(mask, dot(a, v, 1, 1), 0.0).astype(BF)
            grad_q = dot(mixed, k, 1, 0) + dot(a, prior, 1, 1)
            grad_k = dot(mixed, q, 0, 0) + dot(v, rest, 1, 1)
            grad_v = dot(scores, a, 0, 0) + dot(k, rest, 1, 0)
            dq[:, head(h, dq_at)] = (grad_q * slope(qu)).astype(BF)
            dkv[:, at] = (grad_k * slope(ku)).astype(BF)
            dkv[:, vat] = grad_v.astype(BF)
            return 0

        lax.fori_loop(0, 2, step, 0)


def turn_kernel(tok_own, tok_sib, out):
    def step(n, _):
        at = pl.ds(pl.multiple_of(n * HD, HD), HD)
        out[n, :, :256] = tok_own[:, at].T
        out[n, :, 256:] = tok_sib[:, at].T
        return 0

    lax.fori_loop(0, 16, step, 0)


def partial_kernel(tok, dkv_own, back, *outs):
    y, x = lax.axis_index("y"), lax.axis_index("x")
    for half in range(2):
        at = slice(half * 256, half * 256 + 256)
        grad = jnp.concatenate([dkv_own[:, at], back[:, at]], axis=0)
        for d in (2, 1, 3, 0):
            out = outs[half * 4 + d]
            to = lax.rem((y if half else x) + d, 4)

            def step(n, _):
                chip = to * 4 + n if half else n * 4 + to
                out[n] = dot(tok[chip], grad, 1, 0).astype(out.dtype)
                return 0

            lax.fori_loop(0, 4, step, 0)


def plane_kernel(*refs):
    for half, axis in ((0, "y"), (1, "x")):
        ins, outs = refs[half * 4 : half * 4 + 4], refs[half * 4 - 8 : len(refs) + half * 4 - 4]
        here = lax.axis_index(axis)
        for e in range(4):
            at = lax.rem(here + e, 4)
            total = ins[0][at]
            for r in ins[1:]:
                total = total + r[at].astype(F32)
            outs[e][...] = total.astype(outs[e].dtype)


def column_kernel(*refs):
    out = refs[-1]
    for half in range(2):
        total = refs[half * 4][...]
        for r in refs[half * 4 + 1 : half * 4 + 4]:
            total = total + r[...].astype(F32)
        out[:, :, half * 256 : half * 256 + 256] = total.reshape(16, 8, 256).astype(BF)


def last_kernel(scale, *refs):
    out = refs[-1]
    for group, parts in enumerate(refs[:2]):
        for c in range(2):
            total = parts[c * 8].astype(F32)
            for k in range(1, 8):
                total = total + parts[c * 8 + k].astype(F32)
            total = total * scale
            for half in range(2):
                at = half * 1024 + c * 512 + group * 256
                out[:, at : at + 256] = total[:, half * 256 : half * 256 + 256]


def token_kernel(*refs):
    dkv, got, o, dq, w, w_sib = (refs[2 * k : 2 * k + 2] for k in range(6))
    out, o_out, dq_out = refs[-3:]
    total = jnp.zeros(out.shape, F32)
    for g in range(2):
        total += dot(dkv[g][...], w[g][0].reshape(256, 512), 1, 1)
        total += dot(got[g][:, :512], w_sib[g][0].reshape(256, 512), 1, 1)
    out[...] = total.astype(BF)

    @pl.when(pl.program_id(0) == 0)
    def _():
        core = lax.axis_index("core")
        for g in range(2):
            mine = pl.ds(pl.multiple_of(core * 512 + g * 256, 256), 256)
            other = pl.ds(pl.multiple_of((1 - core) * 512 + g * 256, 256), 256)
            o_out[:, mine] = o[g][...]
            o_out[:, other] = got[g][:, 768:]
            dq_out[:, mine] = dq[g][...]
            dq_out[:, other] = got[g][:, 512:768]


def token_call(rows, *args):
    def fixed(shape):
        return pl.BlockSpec(shape, lambda n: (0,) * len(shape))

    tile = pl.BlockSpec((1, 16, 16, 512), lambda n: (n, 0, 0, 0))
    return pl.pallas_call(
        token_kernel,
        grid=(8,),
        out_shape=[jax.ShapeDtypeStruct((rows, n), BF) for n in (2048, 1024, 1024)],
        in_specs=[fixed(a.shape) for a in args[:8]] + [tile] * 4,
        out_specs=[pl.BlockSpec((rows, 256), lambda n: (0, n))] + [fixed((rows, 1024))] * 2,
        cost_estimate=pl.CostEstimate(
            flops=4 * 2 * rows * 2048 * 2048, bytes_accessed=12 << 20, transcendentals=0
        ),
    )(*args)


def on_device(tokens, queries, kv_weight, out_grad):
    rows = tokens.shape[0]
    core = lax.axis_index("core")

    def swap(x):
        return lax.ppermute(x, "core", [(0, 1), (1, 0)])

    def theirs(x):
        return swap(lax.dynamic_slice_in_dim(x, (1 - core) * 512, 512, 1))

    place = lax.axis_index(("y", "x"))
    mine = lax.dynamic_slice_in_dim(kv_weight, place * 16, 16, 0).reshape(16, 2, 2, 512)
    mine = lax.dynamic_index_in_dim(mine, core, 2, keepdims=False).reshape(16, 1024)
    along_z = lax.all_to_all(jnp.broadcast_to(mine[None], (8, 16, 1024)), "z", 0, 0, tiled=True)
    a0, b0 = along_z[:, :, :512], along_z[:, :, 512:]
    (a2, b2), (a1, b1), (a3, b3) = [(shift(a0, "x", d), shift(b0, "y", d)) for d in (2, 1, 3)]
    pieces = []
    for g in range(2):
        at = slice(g * 256, g * 256 + 256)
        a = jnp.stack([p[:, :, at] for p in (a0, a1, a2, a3)])
        b = jnp.stack([p[:, :, at] for p in (b0, b1, b2, b3)])
        (p2, r2), (p1, r1), (p3, r3) = [(shift(a, "y", e), shift(b, "x", e)) for e in (2, 1, 3)]
        pieces.append((a, p1, p2, p3, b, r1, r2, r3))

    sib_tokens = swap(tokens)
    sib_q, sib_g = theirs(queries), theirs(out_grad)
    (turned,) = call(turn_kernel, [((16, HD, 2 * rows), BF)], tokens, sib_tokens)
    half = ((rows, 256), BF)
    whole = ((rows, 512), BF)
    states = ((4, HD, HD), BF)
    groups = range(2)

    def exchange(x, later):
        x = lax.all_to_all(x.reshape(8, 64, HD), "z", 0, 0, tiled=True)
        (x,) = call(lambda i, o: sums_kernel(later, i, o), [((8, 64, HD), BF)], x)
        return lax.all_to_all(x, "z", 0, 0, tiled=True).reshape(4, HD, HD)

    def key_value(g):
        return call(
            key_value_kernel,
            [((8, 16, 16, 512), BF), whole, whole, states],
            tokens, sib_tokens, *pieces[g], turned,
            in_specs=[VMEM] * 2 + [ANY] * 9,
            scratch=[pltpu.SemaphoreType.DMA((32,))],
            flops=2 * 512 * 2048 * 512,
        )

    def forward(g):
        return call(
            functools.partial(forward_kernel, g),
            [half, half, half, half, states],
            queries, sib_q, out_grad, sib_g, kv[g][1], kv[g][2], before[g],
            flops=2 * 4 * 256 * 128 * 768,
        )

    def backward(g, *ahead):
        args = (queries, sib_q, *kv[g][1:3], *fw[g][2:4], fw[g][1], before[g], after[g])
        return call(
            functools.partial(backward_kernel, g),
            [half, whole, ((rows, 1024), BF)],
            *args, *ahead,
            in_specs=[VMEM] * len(args) + [ANY] * len(ahead),
            flops=2 * 4 * 256 * 128 * 1664,
        )

    def partial(g):
        full, sent = ((4, 128, 256), F32), ((4, 128, 256), BF)
        return call(
            partial_kernel,
            [full, sent, sent, sent, full, sent, sent, sent],
            turned, bw[g][1], bw[g][2],
            flops=2 * 512 * 2048 * 512,
        )

    def spread(parts, first, second):
        a, b = {}, {}
        for d in (2, 1, 3):
            a[d], b[d] = shift(parts[d], first, d), shift(parts[4 + d], second, d)
        return parts[0], a[1], a[2], a[3], parts[4], b[1], b[2], b[3]

    kv = [key_value(g) for g in groups]
    sib_w = [swap(kv[g][0]) for g in groups]
    before = [exchange(kv[g][3], False) for g in groups]
    fw = [forward(g) for g in groups]
    after = [exchange(fw[g][4], True) for g in groups]
    bw = [backward(0)]
    parts = [partial(0)]
    bw.append(backward(1, parts[0][7]))
    parts.append(partial(1))
    got = [swap(bw[g][2]) for g in groups]
    token_grad, output, query_grad = token_call(
        rows, *(bw[g][1] for g in groups), *got, *(fw[g][0] for g in groups),
        *(bw[g][0] for g in groups), *(kv[g][0] for g in groups), *sib_w,
    )
    full, sent = ((128, 256), F32), ((128, 256), BF)
    columns = []
    for g in groups:
        extra = [token_grad] if g == 1 else [parts[1][7]]
        sums = call(
            plane_kernel,
            [full, sent, sent, sent, full, sent, sent, sent],
            *spread(parts[g], "x", "y"), *extra,
            in_specs=[VMEM] * 8 + [ANY] * len(extra),
        )
        sums = spread(sums, "y", "x")
        (column,) = call(column_kernel, [((16, 8, 512), BF)], *sums)
        columns.append(lax.all_to_all(column, ("core", "z"), 0, 0, tiled=True))
    scale = 1.0 / math.sqrt(rows * lax.axis_size(("y", "x", "core", "z")))
    (weight_grad,) = call(
        functools.partial(last_kernel, scale), [((8, 2048), F32)], *columns
    )
    return (output, token_grad, query_grad, weight_grad)


def solution(mesh):
    fine = Mesh(mesh.devices.reshape(4, 4, 2, 8), ("y", "x", "core", "z"))
    rows = P(("y", "x", "core", "z"), None)
    return jax.shard_map(
        on_device,
        mesh=fine,
        in_specs=(rows, rows, P("z", None), rows),
        out_specs=(rows, rows, rows, rows),
        check_vma=False,
    )
```

```python
import functools
import math

import jax
import jax.numpy as jnp
from jax import lax
from jax.experimental import pallas as pl
from jax.experimental.pallas import tpu as pltpu
from jax.sharding import Mesh
from jax.sharding import PartitionSpec as P

HD = 128
EPSILON = 1e-05
BF = jnp.bfloat16
F32 = jnp.float32
VMEM = pl.BlockSpec(memory_space=pltpu.VMEM)
ANY = pl.BlockSpec(memory_space=pl.ANY)


def feature(u):
    return jnp.where(u > 0, u + 1.0, jnp.exp(jnp.minimum(u, 0.0)))


def slope(u):
    return jnp.where(u > 0, 1.0, jnp.exp(jnp.minimum(u, 0.0)))


def dot(a, b, da, db):
    return lax.dot_general(a, b, (((da,), (db,)), ((), ())), preferred_element_type=F32)


def call(body, outs, *args, in_specs=None, scratch=(), flops=0):
    size = sum(math.prod(a.shape) * a.dtype.itemsize for a in args)
    size += sum(math.prod(s) * jnp.dtype(d).itemsize for s, d in outs)
    return pl.pallas_call(
        body,
        out_shape=[jax.ShapeDtypeStruct(s, d) for s, d in outs],
        in_specs=in_specs or [VMEM] * len(args),
        out_specs=[VMEM] * len(outs),
        scratch_shapes=list(scratch),
        cost_estimate=pl.CostEstimate(flops=flops, bytes_accessed=size, transcendentals=0),
    )(*args)


def shift(x, axis, step):
    size = lax.axis_size(axis)
    return lax.ppermute(x, axis, [(i, (i + step) % size) for i in range(size)])


def turn_kernel(own, sib, both, turned):
    both[:256] = own[...]
    both[256:] = sib[...]
    for n in range(16):
        at = slice(n * HD, n * HD + HD)
        turned[n, :, :256] = own[:, at].T
        turned[n, :, 256:] = sib[:, at].T


def key_value_kernel(tok, *refs):
    pieces, (w_ref, kv, state), sems = refs[:8], refs[-4:-1], refs[-1]
    y, x = lax.axis_index("y"), lax.axis_index("x")
    copies = []
    for half in range(2):
        for e in range(4):
            for d in range(4):
                py, px = (y - e, x - d) if half == 0 else (y - d, x - e)
                place = lax.rem(py + 4, 4) * 4 + lax.rem(px + 4, 4)
                copies.append(
                    pltpu.make_async_copy(
                        pieces[half * 4 + e].at[d],
                        w_ref.at[:, place, :, pl.ds(half * 512, 512)],
                        sems.at[len(copies)],
                    )
                )
    for c in copies:
        c.start()
    for half in range(2):
        for c in copies[half * 16 : half * 16 + 16]:
            c.wait()

        def tile(n, _):
            at = pl.ds(pl.multiple_of(n * 256, 256), 256)
            w = w_ref[:, :, :, at].reshape(2048, 256)
            kv[:, at] = dot(tok[...], w, 1, 0).astype(BF)
            return 0

        lax.fori_loop(half * 2, half * 2 + 2, tile, 0)
    for s in range(2):
        rows = slice(s * 256, s * 256 + 256)
        for h in range(4):
            k = feature(kv[rows, h * HD : (h + 1) * HD].astype(F32)).astype(BF)
            v = kv[rows, 512 + h * HD : 512 + (h + 1) * HD]
            state[s * 4 + h] = dot(k, v, 0, 0).astype(BF)


def sums_kernel(later, states, out):
    order = list(range(states.shape[0]))
    if later:
        order.reverse()
    total = jnp.zeros(states.shape[1:], F32)
    for k in order:
        out[k] = total.astype(BF)
        total = total + states[k].astype(F32)


def causal():
    shape = (256, 256)
    return lax.broadcasted_iota(jnp.int32, shape, 0) >= lax.broadcasted_iota(jnp.int32, shape, 1)


def spots():
    for s in range(2):
        for h in range(4):
            rows = slice(s * 256, s * 256 + 256)
            yield (
                s * 4 + h,
                rows,
                slice(h * HD, (h + 1) * HD),
                slice(512 + h * HD, 512 + (h + 1) * HD),
            )


def local_kernel(q_own, q_sib, kv, qu, scores, local):
    mask = causal()
    at = lax.axis_index("core") * 512
    qu[:256] = q_own[:, pl.ds(pl.multiple_of(at, 512), 512)]
    qu[256:] = q_sib[...]
    for n, rows, at, vat in spots():
        q = feature(qu[rows, at].astype(F32)).astype(BF)
        k = feature(kv[rows, at].astype(F32)).astype(BF)
        score = jnp.where(mask, dot(q, k, 1, 1), 0.0).astype(BF)
        scores[n] = score
        local[rows, at] = dot(score, kv[rows, vat], 1, 0)


def forward_kernel(qu, g_own, g_sib, local, before, out, grad_att, state):
    core = lax.axis_index("core")
    for n, rows, at, _ in spots():
        q = feature(qu[rows, at].astype(F32)).astype(BF)
        attended = local[rows, at] + dot(q, before[n], 1, 0)
        if n < 4:
            g = g_own[:, pl.ds(pl.multiple_of(core * 512 + n * HD, HD), HD)].astype(F32)
        else:
            g = g_sib[:, at].astype(F32)
        power = jnp.mean(attended * attended, axis=-1, keepdims=True) + EPSILON
        inverse = lax.rsqrt(power)
        normed = attended * inverse
        along = jnp.mean(g * normed, axis=-1, keepdims=True)
        grad = ((g - normed * along) * inverse).astype(BF)
        out[rows, at] = normed.astype(BF)
        grad_att[rows, at] = grad
        state[n] = dot(q, grad, 0, 0).astype(BF)


def mixed_kernel(qu, kv, scores, grad_att, before, dq, local):
    mask = causal()
    for n, rows, at, vat in spots():
        u = qu[rows, at].astype(F32)
        q = feature(u).astype(BF)
        k = feature(kv[rows, at].astype(F32)).astype(BF)
        a = grad_att[rows, at]
        mixed = jnp.where(mask, dot(a, kv[rows, vat], 1, 1), 0.0).astype(BF)
        grad_q = dot(mixed, k, 1, 0) + dot(a, before[n], 1, 1)
        dq[rows, at] = (grad_q * slope(u)).astype(BF)
        local[rows, at] = dot(mixed, q, 0, 0)
        local[rows, vat] = dot(scores[n], a, 0, 0)


def backward_kernel(kv, local, after, dkv):
    for n, rows, at, vat in spots():
        u = kv[rows, at].astype(F32)
        k, v = feature(u).astype(BF), kv[rows, vat]
        grad_k = local[rows, at] + dot(v, after[n], 1, 1)
        grad_v = local[rows, vat] + dot(k, after[n], 1, 0)
        dkv[rows, at] = (grad_k * slope(u)).astype(BF)
        dkv[rows, vat] = grad_v.astype(BF)


def pack_kernel(dkv, dq, out, _, back):
    back[:, :1024] = dkv[256:]
    back[:, 1024:1536] = dq[256:]
    back[:, 1536:] = out[256:]


def partial_kernel(steps, turned, dkv, *outs):
    y, x = lax.axis_index("y"), lax.axis_index("x")
    for i, d in enumerate(steps):
        tx, ty = lax.rem(x + d, 4), lax.rem(y + d, 4)
        tok = jnp.concatenate([turned[n * 4 + tx] for n in range(4)], axis=0)
        outs[2 * i][...] = dot(tok, dkv[:, :512], 1, 0).astype(BF).reshape(4, 128, 512)
        tok = turned[pl.ds(ty * 4, 4)].reshape(512, 512)
        outs[2 * i + 1][...] = dot(tok, dkv[:, 512:], 1, 0).astype(BF).reshape(4, 128, 512)


def plane_kernel(*refs):
    outs = refs[-8:]
    for half, axis in ((0, "y"), (1, "x")):
        here = lax.axis_index(axis)
        for e in range(4):
            at = lax.rem(here + e, 4)
            total = refs[half * 4][at].astype(F32)
            for r in refs[half * 4 + 1 : half * 4 + 4]:
                total = total + r[at].astype(F32)
            to = outs[half * 4 + e]
            to[...] = total.astype(to.dtype)


def column_kernel(*refs):
    out = refs[-1]
    for half in range(2):
        total = refs[half * 4][...]
        for r in refs[half * 4 + 1 : half * 4 + 4]:
            total = total + r[...].astype(F32)
        out[:, :, half * 512 : half * 512 + 512] = total.reshape(16, 8, 512).astype(BF)


def last_kernel(scale, parts, out):
    for c in range(2):
        total = parts[c * 8].astype(F32)
        for k in range(1, 8):
            total = total + parts[c * 8 + k].astype(F32)
        total = total * scale
        for half in range(2):
            at = half * 1024 + c * 512
            out[:, at : at + 512] = total[:, half * 512 : half * 512 + 512]


def token_kernel(dkv, got, o, dq, w, w_sib, out, o_out, dq_out):
    total = dot(dkv[:256], w[0].reshape(256, 1024), 1, 1)
    total += dot(got[:, :1024], w_sib[0].reshape(256, 1024), 1, 1)
    out[...] = total.astype(BF)

    @pl.when(pl.program_id(0) == 0)
    def _():
        core = lax.axis_index("core")
        mine = pl.ds(pl.multiple_of(core * 512, 512), 512)
        other = pl.ds(pl.multiple_of((1 - core) * 512, 512), 512)
        o_out[:, mine] = o[:256]
        o_out[:, other] = got[:, 1536:]
        dq_out[:, mine] = dq[:256]
        dq_out[:, other] = got[:, 1024:1536]


def token_call(rows, *args):
    def fixed(shape):
        return pl.BlockSpec(shape, lambda n: (0,) * len(shape))

    tile = pl.BlockSpec((1, 16, 16, 1024), lambda n: (n, 0, 0, 0))
    return pl.pallas_call(
        token_kernel,
        grid=(8,),
        out_shape=[jax.ShapeDtypeStruct((rows, n), BF) for n in (2048, 1024, 1024)],
        in_specs=[fixed(a.shape) for a in args[:4]] + [tile] * 2,
        out_specs=[pl.BlockSpec((rows, 256), lambda n: (0, n))] + [fixed((rows, 1024))] * 2,
        cost_estimate=pl.CostEstimate(
            flops=4 * 2 * rows * 2048 * 2048, bytes_accessed=12 << 20, transcendentals=0
        ),
    )(*args)


def on_device(tokens, queries, kv_weight, out_grad):
    rows = tokens.shape[0]
    core = lax.axis_index("core")

    def swap(x):
        return lax.ppermute(x, "core", [(0, 1), (1, 0)])

    def theirs(x):
        return swap(lax.dynamic_slice_in_dim(x, (1 - core) * 512, 512, 1))

    place = lax.axis_index(("y", "x"))
    mine = lax.dynamic_slice_in_dim(kv_weight, place * 16, 16, 0).reshape(16, 2, 2, 512)
    mine = lax.dynamic_index_in_dim(mine, core, 2, keepdims=False).reshape(16, 1024)
    along_z = lax.all_to_all(jnp.broadcast_to(mine[None], (8, 16, 1024)), "z", 0, 0, tiled=True)
    a0, b0 = along_z[:, :, :512], along_z[:, :, 512:]
    first = [(shift(a0, "x", d), shift(b0, "y", d)) for d in (2, 1, 3)]
    (a2, b2), (a1, b1), (a3, b3) = first
    a = jnp.stack([a0, a1, a2, a3])
    b = jnp.stack([b0, b1, b2, b3])
    (p2, r2), (p1, r1), (p3, r3) = [(shift(a, "y", e), shift(b, "x", e)) for e in (2, 1, 3)]

    sib_tokens = swap(tokens)
    sib_q, sib_g = theirs(queries), theirs(out_grad)
    both, turned = call(
        turn_kernel,
        [((2 * rows, 2048), BF), ((16, HD, 2 * rows), BF)],
        tokens, sib_tokens,
    )
    half = ((2 * rows, 512), BF)
    whole = ((2 * rows, 1024), BF)
    states = ((8, HD, HD), BF)
    w, kv, state = call(
        key_value_kernel,
        [((8, 16, 16, 1024), BF), whole, states],
        both, a, p1, p2, p3, b, r1, r2, r3,
        in_specs=[VMEM] + [ANY] * 8,
        scratch=[pltpu.SemaphoreType.DMA((32,))],
        flops=2 * 512 * 2048 * 1024,
    )
    sib_w = swap(w)

    def exchange(x, later, ahead):
        x = lax.all_to_all(x, "z", 0, 0, tiled=True)
        (x,) = call(
            lambda i, _, o: sums_kernel(later, i, o), [states], x, ahead, in_specs=[VMEM, ANY]
        )
        return lax.all_to_all(x, "z", 0, 0, tiled=True)

    qu, scores, local = call(
        local_kernel,
        [half, ((8, 256, 256), BF), ((2 * rows, 512), F32)],
        queries, sib_q, kv,
        flops=2 * 8 * 256 * 256 * 256,
    )
    before = exchange(state, False, local)
    out, grad_att, state = call(
        forward_kernel,
        [half, half, states],
        qu, out_grad, sib_g, local, before,
        flops=2 * 8 * 256 * 128 * 256,
    )
    dq, local = call(
        mixed_kernel,
        [half, ((2 * rows, 1024), F32)],
        qu, kv, scores, grad_att, before,
        flops=2 * 8 * 256 * 256 * 640,
    )
    after = exchange(state, True, local)
    (dkv,) = call(
        backward_kernel, [whole], kv, local, after, flops=2 * 8 * 256 * 128 * 256
    )

    def partial(*steps):
        return call(
            functools.partial(partial_kernel, steps),
            [((4, 128, 512), BF)] * (2 * len(steps)),
            turned, dkv,
            flops=2 * 512 * 512 * 1024 * len(steps),
        )

    far_a, far_b = partial(2)
    a1, b1, a3, b3 = partial(1, 3)
    wa = {2: shift(far_a, "x", 2), 1: shift(a1, "x", 1), 3: shift(a3, "x", 3)}
    wb = {2: shift(far_b, "y", 2), 1: shift(b1, "y", 1), 3: shift(b3, "y", 3)}
    a0, b0 = partial(0)
    (back,) = call(
        pack_kernel, [((rows, 2048), BF)], dkv, dq, out, far_a, in_specs=[VMEM] * 3 + [ANY]
    )
    token_grad, output, query_grad = token_call(rows, dkv, swap(back), out, dq, w, sib_w)
    full = ((128, 512), F32)
    sent = ((128, 512), BF)
    parts = call(
        plane_kernel,
        [full, sent, sent, sent, full, sent, sent, sent],
        a0, wa[1], wa[2], wa[3], b0, wb[1], wb[2], wb[3], token_grad,
        in_specs=[VMEM] * 8 + [ANY],
    )
    wa, wb = {}, {}
    for d in (2, 1, 3):
        wa[d], wb[d] = shift(parts[d], "y", d), shift(parts[4 + d], "x", d)
    (column,) = call(
        column_kernel,
        [((16, 8, 1024), BF)],
        parts[0], wa[1], wa[2], wa[3], parts[4], wb[1], wb[2], wb[3],
    )
    column = lax.all_to_all(column, ("core", "z"), 0, 0, tiled=True)
    scale = 1.0 / math.sqrt(rows * lax.axis_size(("y", "x", "core", "z")))
    (weight_grad,) = call(lambda i, o: last_kernel(scale, i, o), [((8, 2048), F32)], column)
    return (output, token_grad, query_grad, weight_grad)


def solution(mesh):
    fine = Mesh(mesh.devices.reshape(4, 4, 2, 8), ("y", "x", "core", "z"))
    rows = P(("y", "x", "core", "z"), None)
    return jax.shard_map(
        on_device,
        mesh=fine,
        in_specs=(rows, rows, P("z", None), rows),
        out_specs=(rows, rows, rows, rows),
        check_vma=False,
    )
```

```python
import math

import jax
import jax.numpy as jnp
from jax import lax
from jax.experimental import pallas as pl
from jax.experimental.pallas import tpu as pltpu
from jax.sharding import Mesh
from jax.sharding import PartitionSpec as P


HD = 128
EPSILON = 1e-05
BF = jnp.bfloat16
F32 = jnp.float32
VMEM = pl.BlockSpec(memory_space=pltpu.VMEM)
ANY = pl.BlockSpec(memory_space=pl.ANY)


def feature(u):
    return jnp.where(u > 0, u + 1.0, jnp.exp(jnp.minimum(u, 0.0)))


def slope(u):
    return jnp.where(u > 0, 1.0, jnp.exp(jnp.minimum(u, 0.0)))


def dot(a, b, da, db):
    return lax.dot_general(a, b, (((da,), (db,)), ((), ())), preferred_element_type=F32)


def call(body, outs, *args, in_specs=None, out_specs=None, scratch=(), flops=0):
    size = sum(math.prod(a.shape) * a.dtype.itemsize for a in args)
    size += sum(math.prod(s) * jnp.dtype(d).itemsize for s, d in outs)
    return pl.pallas_call(
        body,
        out_shape=[jax.ShapeDtypeStruct(s, d) for s, d in outs],
        in_specs=in_specs or [VMEM] * len(args),
        out_specs=out_specs or [VMEM] * len(outs),
        scratch_shapes=list(scratch),
        cost_estimate=pl.CostEstimate(flops=flops, bytes_accessed=size, transcendentals=0),
    )(*args)


def shift(x, axis, step):
    size = lax.axis_size(axis)
    return lax.ppermute(x, axis, [(i, (i + step) % size) for i in range(size)])


def turn_kernel(own, sib, both, turned):
    both[:256] = own[...]
    both[256:] = sib[...]
    for n in range(16):
        at = slice(n * HD, n * HD + HD)
        turned[n, :, :256] = own[:, at].T
        turned[n, :, 256:] = sib[:, at].T


def key_value_kernel(tok, *refs):
    pieces, (w_out, kv, state, w_ref, sems, out_sems) = refs[:8], refs[8:]
    y, x = lax.axis_index("y"), lax.axis_index("x")
    copies = []
    for half in range(2):
        for e in range(4):
            for d in range(4):
                py, px = (y - e, x - d) if half == 0 else (y - d, x - e)
                place = lax.rem(py + 4, 4) * 4 + lax.rem(px + 4, 4)
                copies.append(
                    pltpu.make_async_copy(
                        pieces[half * 4 + e].at[d],
                        w_ref.at[:, place, :, pl.ds(half * 512, 512)],
                        sems.at[len(copies)],
                    )
                )
    for c in copies:
        c.start()
    stored = []
    for half in range(2):
        for c in copies[half * 16 : half * 16 + 16]:
            c.wait()
        at = pl.ds(half * 512, 512)
        stored.append(
            pltpu.make_async_copy(
                w_ref.at[:, :, :, at], w_out.at[:, :, :, at], out_sems.at[half]
            )
        )
        stored[-1].start()

        def tile(n, _):
            at = pl.ds(pl.multiple_of(n * 256, 256), 256)
            w = w_ref[:, :, :, at].reshape(2048, 256)
            kv[:, at] = dot(tok[...], w, 1, 0).astype(BF)
            return 0

        lax.fori_loop(half * 2, half * 2 + 2, tile, 0)
    for s in range(2):
        rows = slice(s * 256, s * 256 + 256)
        for h in range(4):
            k = feature(kv[rows, h * HD : (h + 1) * HD].astype(F32)).astype(BF)
            v = kv[rows, 512 + h * HD : 512 + (h + 1) * HD]
            state[s * 4 + h] = dot(k, v, 0, 0).astype(BF)
    for c in stored:
        c.wait()


def sums_kernel(later, states, out):
    order = list(range(states.shape[0]))
    if later:
        order.reverse()
    total = jnp.zeros(states.shape[1:], F32)
    for k in order:
        out[k] = total.astype(BF)
        total = total + states[k].astype(F32)


def causal():
    shape = (256, 256)
    return lax.broadcasted_iota(jnp.int32, shape, 0) >= lax.broadcasted_iota(jnp.int32, shape, 1)


def spots():
    for s in range(2):
        for h in range(4):
            rows = slice(s * 256, s * 256 + 256)
            yield (
                s * 4 + h,
                rows,
                slice(h * HD, (h + 1) * HD),
                slice(512 + h * HD, 512 + (h + 1) * HD),
            )


def local_kernel(q_own, q_sib, kv, qu, qf, scores, local):
    mask = causal()
    at = lax.axis_index("core") * 512
    qu[:256] = q_own[:, pl.ds(pl.multiple_of(at, 512), 512)]
    qu[256:] = q_sib[...]
    for n, rows, at, vat in spots():
        q = feature(qu[rows, at].astype(F32)).astype(BF)
        qf[rows, at] = q
        k = feature(kv[rows, at].astype(F32)).astype(BF)
        score = jnp.where(mask, dot(q, k, 1, 1), 0.0).astype(BF)
        scores[n] = score
        local[rows, at] = dot(score, kv[rows, vat], 1, 0)


def forward_kernel(qf, g_own, g_sib, local, before, out, grad_att, state):
    core = lax.axis_index("core")
    for n, rows, at, _ in spots():
        q = qf[rows, at]
        attended = local[rows, at] + dot(q, before[n], 1, 0)
        if n < 4:
            g = g_own[:, pl.ds(pl.multiple_of(core * 512 + n * HD, HD), HD)].astype(F32)
        else:
            g = g_sib[:, at].astype(F32)
        power = jnp.mean(attended * attended, axis=-1, keepdims=True) + EPSILON
        inverse = lax.rsqrt(power)
        normed = attended * inverse
        along = jnp.mean(g * normed, axis=-1, keepdims=True)
        grad = ((g - normed * along) * inverse).astype(BF)
        out[rows, at] = normed.astype(BF)
        grad_att[rows, at] = grad
        state[n] = dot(q, grad, 0, 0).astype(BF)


def mixed_kernel(qu, qf, kv, scores, grad_att, before, dq, local):
    mask = causal()
    for n, rows, at, vat in spots():
        u, q = qu[rows, at].astype(F32), qf[rows, at]
        k = feature(kv[rows, at].astype(F32)).astype(BF)
        a = grad_att[rows, at]
        mixed = jnp.where(mask, dot(a, kv[rows, vat], 1, 1), 0.0).astype(BF)
        grad_q = dot(mixed, k, 1, 0) + dot(a, before[n], 1, 1)
        dq[rows, at] = (grad_q * slope(u)).astype(BF)
        local[rows, at] = dot(mixed, q, 0, 0)
        local[rows, vat] = dot(scores[n], a, 0, 0)


def chunk(half, d, turned, dkv):
    if half == 0:
        to = lax.rem(lax.axis_index("x") + d, 4)
        tok = jnp.concatenate([turned[n * 4 + to] for n in range(4)], axis=0)
    else:
        to = lax.rem(lax.axis_index("y") + d, 4)
        tok = turned[pl.ds(to * 4, 4)].reshape(512, 512)
    part = dot(tok, dkv[:, half * 512 : half * 512 + 512], 1, 0)
    return part.astype(BF).reshape(4, 128, 512)


STEPS = (2, 1, 3)


def backward_kernel(kv, local, after, turned_hbm, dkv, *refs):
    outs, (turned, held, sem, sems) = refs[:6], refs[6:]
    load = pltpu.make_async_copy(turned_hbm, turned, sem)
    load.start()
    for n, rows, at, vat in spots():
        u = kv[rows, at].astype(F32)
        k, v = feature(u).astype(BF), kv[rows, vat]
        grad_k = local[rows, at] + dot(v, after[n], 1, 1)
        grad_v = local[rows, vat] + dot(k, after[n], 1, 0)
        dkv[rows, at] = (grad_k * slope(u)).astype(BF)
        dkv[rows, vat] = grad_v.astype(BF)
    load.wait()
    stores = []
    for i, d in enumerate(STEPS):
        for half in range(2):
            n = 2 * i + half
            held[n] = chunk(half, d, turned, dkv)
            stores.append(pltpu.make_async_copy(held.at[n], outs[n], sems.at[n]))
            stores[-1].start()
    for c in stores:
        c.wait()


def own_kernel(turned, dkv, _, a_ref, b_ref):
    a_ref[...] = chunk(0, 0, turned, dkv)
    b_ref[...] = chunk(1, 0, turned, dkv)


def pack_kernel(dkv, dq, out, _, back):
    back[:, :1024] = dkv[256:]
    back[:, 1024:1536] = dq[256:]
    back[:, 1536:] = out[256:]


def plane_kernel(*refs):
    ins, outs, (held, sems) = refs[:8], refs[9:17], refs[17:]
    y, x = lax.axis_index("y"), lax.axis_index("x")
    loads = {}
    for e in (2, 1, 3, 0):
        for half, here in ((0, y), (1, x)):
            at = lax.rem(here + e, 4)
            for k in range(4):
                n = (e * 2 + half) * 4 + k
                loads[n] = pltpu.make_async_copy(ins[half * 4 + k].at[at], held.at[n], sems.at[n])
                loads[n].start()
    for e in (2, 1, 3, 0):
        for half in range(2):
            first = (e * 2 + half) * 4
            for n in range(first, first + 4):
                loads[n].wait()
            total = held[first].astype(F32)
            for n in range(first + 1, first + 4):
                total = total + held[n].astype(F32)
            to = outs[half * 4 + e]
            to[...] = total.astype(to.dtype)


def column_kernel(*refs):
    out = refs[-1]
    for half in range(2):
        total = refs[half * 4][...]
        for r in refs[half * 4 + 1 : half * 4 + 4]:
            total = total + r[...].astype(F32)
        out[:, :, half * 512 : half * 512 + 512] = total.reshape(16, 8, 512).astype(BF)


def last_kernel(scale, parts, out):
    for c in range(2):
        total = parts[c * 8].astype(F32)
        for k in range(1, 8):
            total = total + parts[c * 8 + k].astype(F32)
        total = total * scale
        for half in range(2):
            at = half * 1024 + c * 512
            out[:, at : at + 512] = total[:, half * 512 : half * 512 + 512]


def token_kernel(dkv, got, o, dq, w, w_sib, out, o_out, dq_out):
    total = dot(dkv[:256], w[0].reshape(256, 1024), 1, 1)
    total += dot(got[:, :1024], w_sib[0].reshape(256, 1024), 1, 1)
    out[...] = total.astype(BF)

    @pl.when(pl.program_id(0) == 0)
    def _():
        core = lax.axis_index("core")
        mine = pl.ds(pl.multiple_of(core * 512, 512), 512)
        other = pl.ds(pl.multiple_of((1 - core) * 512, 512), 512)
        o_out[:, mine] = o[:256]
        o_out[:, other] = got[:, 1536:]
        dq_out[:, mine] = dq[:256]
        dq_out[:, other] = got[:, 1024:1536]


def token_call(rows, *args):
    def fixed(shape):
        return pl.BlockSpec(shape, lambda n: (0,) * len(shape))

    tile = pl.BlockSpec((1, 16, 16, 1024), lambda n: (n, 0, 0, 0))
    return pl.pallas_call(
        token_kernel,
        grid=(8,),
        out_shape=[jax.ShapeDtypeStruct((rows, n), BF) for n in (2048, 1024, 1024)],
        in_specs=[fixed(a.shape) for a in args[:4]] + [tile] * 2,
        out_specs=[pl.BlockSpec((rows, 256), lambda n: (0, n))] + [fixed((rows, 1024))] * 2,
        cost_estimate=pl.CostEstimate(
            flops=4 * 2 * rows * 2048 * 2048, bytes_accessed=12 << 20, transcendentals=0
        ),
    )(*args)


def on_device(tokens, queries, kv_weight, out_grad):
    rows = tokens.shape[0]
    core = lax.axis_index("core")

    def swap(x):
        return lax.ppermute(x, "core", [(0, 1), (1, 0)])

    def theirs(x):
        return swap(lax.dynamic_slice_in_dim(x, (1 - core) * 512, 512, 1))

    place = lax.axis_index(("y", "x"))
    mine = lax.dynamic_slice_in_dim(kv_weight, place * 16, 16, 0).reshape(16, 2, 2, 512)
    mine = lax.dynamic_index_in_dim(mine, core, 2, keepdims=False).reshape(16, 1024)
    along_z = lax.all_to_all(jnp.broadcast_to(mine[None], (8, 16, 1024)), "z", 0, 0, tiled=True)
    a0, b0 = along_z[:, :, :512], along_z[:, :, 512:]
    first = [(shift(a0, "x", d), shift(b0, "y", d)) for d in (2, 1, 3)]
    (a2, b2), (a1, b1), (a3, b3) = first
    a = jnp.stack([a0, a1, a2, a3])
    b = jnp.stack([b0, b1, b2, b3])
    (p2, r2), (p1, r1), (p3, r3) = [(shift(a, "y", e), shift(b, "x", e)) for e in (2, 1, 3)]

    sib_tokens = swap(tokens)
    sib_q, sib_g = theirs(queries), theirs(out_grad)
    both, turned = call(
        turn_kernel,
        [((2 * rows, 2048), BF), ((16, HD, 2 * rows), BF)],
        tokens, sib_tokens,
    )
    half = ((2 * rows, 512), BF)
    whole = ((2 * rows, 1024), BF)
    states = ((8, HD, HD), BF)
    w, kv, state = call(
        key_value_kernel,
        [((8, 16, 16, 1024), BF), whole, states],
        both, a, p1, p2, p3, b, r1, r2, r3,
        in_specs=[VMEM] + [ANY] * 8,
        out_specs=[ANY, VMEM, VMEM],
        scratch=[
            pltpu.VMEM((8, 16, 16, 1024), BF),
            pltpu.SemaphoreType.DMA((32,)),
            pltpu.SemaphoreType.DMA((2,)),
        ],
        flops=2 * 512 * 2048 * 1024,
    )
    sib_w = swap(w)

    def exchange(x, later, ahead):
        x = lax.all_to_all(x, "z", 0, 0, tiled=True)
        (x,) = call(
            lambda i, _, o: sums_kernel(later, i, o), [states], x, ahead, in_specs=[VMEM, ANY]
        )
        return lax.all_to_all(x, "z", 0, 0, tiled=True)

    qu, qf, scores, local = call(
        local_kernel,
        [half, half, ((8, 256, 256), BF), ((2 * rows, 512), F32)],
        queries, sib_q, kv,
        flops=2 * 8 * 256 * 256 * 256,
    )
    before = exchange(state, False, local)
    out, grad_att, state = call(
        forward_kernel,
        [half, half, states],
        qf, out_grad, sib_g, local, before,
        flops=2 * 8 * 256 * 128 * 256,
    )
    dq, local = call(
        mixed_kernel,
        [half, ((2 * rows, 1024), F32)],
        qu, qf, kv, scores, grad_att, before,
        flops=2 * 8 * 256 * 256 * 640,
    )
    after = exchange(state, True, local)
    sent = ((4, 128, 512), BF)
    dkv, a2, b2, a1, b1, a3, b3 = call(
        backward_kernel,
        [whole] + [sent] * 6,
        kv, local, after, turned,
        in_specs=[VMEM] * 3 + [ANY],
        out_specs=[VMEM] + [ANY] * 6,
        scratch=[
            pltpu.VMEM((16, HD, 2 * rows), BF),
            pltpu.VMEM((6, 4, 128, 512), BF),
            pltpu.SemaphoreType.DMA(()),
            pltpu.SemaphoreType.DMA((6,)),
        ],
        flops=2 * 512 * 2048 * 1024,
    )
    wa, wb = {}, {}
    for d, to_x, to_y in ((2, a2, b2), (1, a1, b1), (3, a3, b3)):
        wa[d] = shift(to_x, "x", d)
        wb[d] = shift(to_y, "y", d)
    (back,) = call(pack_kernel, [((rows, 2048), BF)], dkv, dq, out, a2, in_specs=[VMEM] * 3 + [ANY])
    a0, b0 = call(
        own_kernel, [sent] * 2, turned, dkv, back, in_specs=[VMEM] * 2 + [ANY],
        flops=2 * 512 * 512 * 1024,
    )
    token_grad, output, query_grad = token_call(rows, dkv, swap(back), out, dq, w, sib_w)
    full = ((128, 512), F32)
    sent = ((128, 512), BF)
    parts = call(
        plane_kernel,
        [full, sent, sent, sent, full, sent, sent, sent],
        a0, wa[1], wa[2], wa[3], b0, wb[1], wb[2], wb[3], token_grad,
        in_specs=[ANY] * 9,
        scratch=[pltpu.VMEM((32, 128, 512), BF), pltpu.SemaphoreType.DMA((32,))],
    )
    wa, wb = {}, {}
    for d in (2, 1, 3):
        wa[d], wb[d] = shift(parts[d], "y", d), shift(parts[4 + d], "x", d)
    (column,) = call(
        column_kernel,
        [((16, 8, 1024), BF)],
        parts[0], wa[1], wa[2], wa[3], parts[4], wb[1], wb[2], wb[3],
    )
    column = lax.all_to_all(column, ("core", "z"), 0, 0, tiled=True)
    scale = 1.0 / math.sqrt(rows * lax.axis_size(("y", "x", "core", "z")))
    (weight_grad,) = call(lambda i, o: last_kernel(scale, i, o), [((8, 2048), F32)], column)
    return (output, token_grad, query_grad, weight_grad)


def solution(mesh):
    fine = Mesh(mesh.devices.reshape(4, 4, 2, 8), ("y", "x", "core", "z"))
    rows = P(("y", "x", "core", "z"), None)
    return jax.shard_map(
        on_device,
        mesh=fine,
        in_specs=(rows, rows, P("z", None), rows),
        out_specs=(rows, rows, rows, rows),
        check_vma=False,
    )
```

```python
import math

import jax
import jax.numpy as jnp
from jax import lax
from jax.experimental import pallas as pl
from jax.experimental.pallas import tpu as pltpu
from jax.sharding import Mesh
from jax.sharding import PartitionSpec as P


HD = 128
EPSILON = 1e-05
BF = jnp.bfloat16
F32 = jnp.float32
VMEM = pl.BlockSpec(memory_space=pltpu.VMEM)
ANY = pl.BlockSpec(memory_space=pl.ANY)


def feature(u):
    return jnp.where(u > 0, u + 1.0, jnp.exp(jnp.minimum(u, 0.0)))


def slope(u):
    return jnp.where(u > 0, 1.0, jnp.exp(jnp.minimum(u, 0.0)))


def dot(a, b, da, db):
    return lax.dot_general(a, b, (((da,), (db,)), ((), ())), preferred_element_type=F32)


def call(body, outs, *args, in_specs=None, out_specs=None, scratch=(), flops=0):
    size = sum(math.prod(a.shape) * a.dtype.itemsize for a in args)
    size += sum(math.prod(s) * jnp.dtype(d).itemsize for s, d in outs)
    return pl.pallas_call(
        body,
        out_shape=[jax.ShapeDtypeStruct(s, d) for s, d in outs],
        in_specs=in_specs or [VMEM] * len(args),
        out_specs=out_specs or [VMEM] * len(outs),
        scratch_shapes=list(scratch),
        cost_estimate=pl.CostEstimate(flops=flops, bytes_accessed=size, transcendentals=0),
    )(*args)


def shift(x, axis, step):
    size = lax.axis_size(axis)
    return lax.ppermute(x, axis, [(i, (i + step) % size) for i in range(size)])


def turn_kernel(own, sib, both, turned):
    both[:256] = own[...]
    both[256:] = sib[...]

    def step(n, _):
        at = pl.ds(pl.multiple_of(n * HD, HD), HD)
        turned[n, :, :256] = own[:, at].T
        turned[n, :, 256:] = sib[:, at].T
        return 0

    lax.fori_loop(0, 16, step, 0)


def project(tok, w_ref, out):
    def tile(n, _):
        at = pl.ds(pl.multiple_of(n * 256, 256), 256)
        if len(w_ref.shape) == 4:
            w = w_ref[:, :, :, at].reshape(2048, 256)
        else:
            w = w_ref[:, :, at].reshape(2048, 256)
        out[:, at] = dot(tok[...], w, 1, 0).astype(BF)
        return 0

    lax.fori_loop(0, 2, tile, 0)


def key_kernel(tok, *refs):
    shards, (w_out, key, w_ref, sems, out_sem) = refs[:9], refs[9:]
    z = lax.axis_index("z")
    copies = []
    for n, step in enumerate((0, -1, 1, -2, 2, -3, 3)):
        to = w_ref.at[lax.rem(z + step + 8, 8)]
        copies.append(pltpu.make_async_copy(shards[n], to, sems.at[n]))
    for n in range(2):
        to = w_ref.at[lax.rem(z + 4, 8), pl.ds(n * 128, 128)]
        copies.append(pltpu.make_async_copy(shards[7 + n], to, sems.at[7 + n]))
    for c in copies:
        c.start()
    for c in copies:
        c.wait()
    store = pltpu.make_async_copy(w_ref, w_out, out_sem)
    store.start()
    project(tok, w_ref, key)
    store.wait()


def value_kernel(tok, key, *refs):
    pieces, (w_out, val, state, w_ref, sems, out_sem) = refs[:8], refs[8:]
    y, x = lax.axis_index("y"), lax.axis_index("x")
    copies = []
    for half in range(2):
        for e in range(4):
            for d in range(4):
                py, px = (y - e, x - d) if half == 0 else (y - d, x - e)
                place = lax.rem(py + 4, 4) * 4 + lax.rem(px + 4, 4)
                copies.append(
                    pltpu.make_async_copy(
                        pieces[half * 4 + e].at[d],
                        w_ref.at[:, place, :, pl.ds(half * 256, 256)],
                        sems.at[len(copies)],
                    )
                )
    for c in copies:
        c.start()
    for c in copies:
        c.wait()
    project(tok, w_ref, val)
    store = pltpu.make_async_copy(w_ref, w_out, out_sem)
    store.start()

    def body(n, rows, at):
        k = feature(key[rows, at].astype(F32)).astype(BF)
        state[n] = dot(k, val[rows, at], 0, 0).astype(BF)

    each_spot(body)
    store.wait()


def sums_kernel(later, states, out):
    order = list(range(states.shape[0]))
    if later:
        order.reverse()
    total = jnp.zeros(states.shape[1:], F32)
    for k in order:
        out[k] = total.astype(BF)
        total = total + states[k].astype(F32)


def causal():
    shape = (256, 256)
    return lax.broadcasted_iota(jnp.int32, shape, 0) >= lax.broadcasted_iota(jnp.int32, shape, 1)


def each_spot(body):
    def step(h, _):
        for s in range(2):
            at = pl.ds(pl.multiple_of(h * HD, HD), HD)
            body(s * 4 + h, slice(s * 256, s * 256 + 256), at)
        return 0

    lax.fori_loop(0, 4, step, 0)


def local_kernel(q_own, q_sib, key, val, qu, qf, scores, local):
    mask = causal()
    at = lax.axis_index("core") * 512
    qu[:256] = q_own[:, pl.ds(pl.multiple_of(at, 512), 512)]
    qu[256:] = q_sib[...]

    def body(n, rows, at):
        q = feature(qu[rows, at].astype(F32)).astype(BF)
        qf[rows, at] = q
        k = feature(key[rows, at].astype(F32)).astype(BF)
        score = jnp.where(mask, dot(q, k, 1, 1), 0.0).astype(BF)
        scores[n] = score
        local[rows, at] = dot(score, val[rows, at], 1, 0)

    each_spot(body)


def forward_kernel(qf, g_own, g_sib, local, before, out, grad_att, state):
    core = lax.axis_index("core")

    def step(h, _):
        at = pl.ds(pl.multiple_of(h * HD, HD), HD)
        mine = pl.ds(pl.multiple_of(core * 512 + h * HD, HD), HD)
        for s, (g_ref, g_at) in enumerate(((g_own, mine), (g_sib, at))):
            n, rows = s * 4 + h, slice(s * 256, s * 256 + 256)
            q, g = qf[rows, at], g_ref[:, g_at].astype(F32)
            attended = local[rows, at] + dot(q, before[n], 1, 0)
            power = jnp.mean(attended * attended, axis=-1, keepdims=True) + EPSILON
            inverse = lax.rsqrt(power)
            normed = attended * inverse
            along = jnp.mean(g * normed, axis=-1, keepdims=True)
            grad = ((g - normed * along) * inverse).astype(BF)
            out[rows, at] = normed.astype(BF)
            grad_att[rows, at] = grad
            state[n] = dot(q, grad, 0, 0).astype(BF)
        return 0

    lax.fori_loop(0, 4, step, 0)


def mixed_kernel(qu, qf, key, val, scores, grad_att, before, dq, local_k, local_v):
    mask = causal()

    def body(n, rows, at):
        u, q = qu[rows, at].astype(F32), qf[rows, at]
        k = feature(key[rows, at].astype(F32)).astype(BF)
        a = grad_att[rows, at]
        mixed = jnp.where(mask, dot(a, val[rows, at], 1, 1), 0.0).astype(BF)
        grad_q = dot(mixed, k, 1, 0) + dot(a, before[n], 1, 1)
        dq[rows, at] = (grad_q * slope(u)).astype(BF)
        local_k[rows, at] = dot(mixed, q, 0, 0)
        local_v[rows, at] = dot(scores[n], a, 0, 0)

    each_spot(body)


def chunk(half, d, turned, dkv):
    if half == 0:
        to = lax.rem(lax.axis_index("x") + d, 4)
        tok = jnp.concatenate([turned[n * 4 + to] for n in range(4)], axis=0)
    else:
        to = lax.rem(lax.axis_index("y") + d, 4)
        tok = turned[pl.ds(to * 4, 4)].reshape(512, 512)
    part = dot(tok, dkv[:, half * 512 : half * 512 + 512], 1, 0)
    return part.astype(BF).reshape(4, 128, 512)


STEPS = (2, 1, 3)


def backward_kernel(key, val, local_k, local_v, after, turned_hbm, dkv, *refs):
    outs, (turned, held, sem, sems) = refs[:6], refs[6:]
    load = pltpu.make_async_copy(turned_hbm, turned, sem)
    load.start()

    def body(n, rows, at):
        u = key[rows, at].astype(F32)
        k, v = feature(u).astype(BF), val[rows, at]
        vat = pl.ds(pl.multiple_of(512 + at.start, HD), HD)
        grad_k = local_k[rows, at] + dot(v, after[n], 1, 1)
        grad_v = local_v[rows, at] + dot(k, after[n], 1, 0)
        dkv[rows, at] = (grad_k * slope(u)).astype(BF)
        dkv[rows, vat] = grad_v.astype(BF)

    each_spot(body)
    load.wait()
    stores = []
    for i, d in enumerate(STEPS):
        for half in range(2):
            n = 2 * i + half
            held[n] = chunk(half, d, turned, dkv)
            stores.append(pltpu.make_async_copy(held.at[n], outs[n], sems.at[n]))
            stores[-1].start()
    for c in stores:
        c.wait()


def own_kernel(turned, dkv, _, a_ref, b_ref):
    a_ref[...] = chunk(0, 0, turned, dkv)
    b_ref[...] = chunk(1, 0, turned, dkv)


def pack_kernel(dkv, dq, out, _, back):
    back[:, :1024] = dkv[256:]
    back[:, 1024:1536] = dq[256:]
    back[:, 1536:] = out[256:]


def plane_kernel(*refs):
    ins, outs, (held, sems) = refs[:8], refs[9:17], refs[17:]
    y, x = lax.axis_index("y"), lax.axis_index("x")
    loads = {}
    for e in (2, 1, 3, 0):
        for half, here in ((0, y), (1, x)):
            at = lax.rem(here + e, 4)
            for k in range(4):
                n = (e * 2 + half) * 4 + k
                loads[n] = pltpu.make_async_copy(ins[half * 4 + k].at[at], held.at[n], sems.at[n])
                loads[n].start()
    for e in (2, 1, 3, 0):
        for half in range(2):
            first = (e * 2 + half) * 4
            for n in range(first, first + 4):
                loads[n].wait()
            total = held[first].astype(F32)
            for n in range(first + 1, first + 4):
                total = total + held[n].astype(F32)
            to = outs[half * 4 + e]
            to[...] = total.astype(to.dtype)


def column_kernel(*refs):
    out = refs[-1]

    def step(n, _):
        rows = pl.ds(pl.multiple_of(n * 64, 64), 64)
        for half in range(2):
            total = refs[half * 4][rows]
            for r in refs[half * 4 + 1 : half * 4 + 4]:
                total = total + r[rows].astype(F32)
            at = slice(half * 512, half * 512 + 512)
            out[pl.ds(n * 8, 8), :, at] = total.reshape(8, 8, 512).astype(BF)
        return 0

    lax.fori_loop(0, 2, step, 0)


def last_kernel(scale, parts, out):
    for c in range(2):
        total = parts[c * 8].astype(F32)
        for k in range(1, 8):
            total = total + parts[c * 8 + k].astype(F32)
        total = total * scale
        for half in range(2):
            at = half * 1024 + c * 512
            out[:, at : at + 512] = total[:, half * 512 : half * 512 + 512]


def token_kernel(dkv, got, o, dq, wk, wk_sib, wv, wv_sib, out, o_out, dq_out):
    total = dot(dkv[:256, :512], wk[0], 1, 1) + dot(got[:, :512], wk_sib[0], 1, 1)
    total += dot(dkv[:256, 512:], wv[0].reshape(128, 512), 1, 1)
    total += dot(got[:, 512:1024], wv_sib[0].reshape(128, 512), 1, 1)
    out[...] = total.astype(BF)

    @pl.when(pl.program_id(0) == 0)
    def _():
        core = lax.axis_index("core")
        mine = pl.ds(pl.multiple_of(core * 512, 512), 512)
        other = pl.ds(pl.multiple_of((1 - core) * 512, 512), 512)
        o_out[:, mine] = o[:256]
        o_out[:, other] = got[:, 1536:]
        dq_out[:, mine] = dq[:256]
        dq_out[:, other] = got[:, 1024:1536]


def token_call(rows, *args):
    def fixed(shape):
        return pl.BlockSpec(shape, lambda n: (0,) * len(shape))

    tile_k = pl.BlockSpec((1, 128, 512), lambda n: (n // 2, n % 2, 0))
    tile_v = pl.BlockSpec((1, 8, 16, 512), lambda n: (n // 2, n % 2, 0, 0))
    return pl.pallas_call(
        token_kernel,
        grid=(16,),
        out_shape=[jax.ShapeDtypeStruct((rows, n), BF) for n in (2048, 1024, 1024)],
        in_specs=[fixed(a.shape) for a in args[:4]] + [tile_k] * 2 + [tile_v] * 2,
        out_specs=[pl.BlockSpec((rows, 128), lambda n: (0, n))] + [fixed((rows, 1024))] * 2,
        cost_estimate=pl.CostEstimate(
            flops=4 * 2 * rows * 2048 * 2048, bytes_accessed=12 << 20, transcendentals=0
        ),
    )(*args)


def on_device(tokens, queries, kv_weight, out_grad):
    rows = tokens.shape[0]
    core = lax.axis_index("core")

    def swap(x):
        return lax.ppermute(x, "core", [(0, 1), (1, 0)])

    def theirs(x):
        return swap(lax.dynamic_slice_in_dim(x, (1 - core) * 512, 512, 1))

    shard = lax.dynamic_slice_in_dim(kv_weight, core * 512, 512, 1)
    shards, left, right = [shard], shard, shard
    for _ in range(3):
        left, right = shift(left, "z", 1), shift(right, "z", -1)
        shards += [left, right]
    shards += [shift(left[:128], "z", 1), shift(right[128:], "z", -1)]
    place = lax.axis_index(("y", "x"))
    mine = lax.dynamic_slice(kv_weight, (place * 16, 1024 + core * 512), (16, 512))
    along_z = lax.all_to_all(jnp.broadcast_to(mine[None], (8, 16, 512)), "z", 0, 0, tiled=True)
    a0, b0 = along_z[:, :, :256], along_z[:, :, 256:]
    (a2, b2), (a1, b1), (a3, b3) = [(shift(a0, "x", d), shift(b0, "y", d)) for d in (2, 1, 3)]
    a = jnp.stack([a0, a1, a2, a3])
    b = jnp.stack([b0, b1, b2, b3])
    (p2, r2), (p1, r1), (p3, r3) = [(shift(a, "y", e), shift(b, "x", e)) for e in (2, 1, 3)]

    sib_tokens = swap(tokens)
    sib_q, sib_g = theirs(queries), theirs(out_grad)
    both, turned = call(
        turn_kernel,
        [((2 * rows, 2048), BF), ((16, HD, 2 * rows), BF)],
        tokens, sib_tokens,
    )
    half = ((2 * rows, 512), BF)
    whole = ((2 * rows, 1024), BF)
    states = ((8, HD, HD), BF)
    w_key, key = call(
        key_kernel,
        [((8, 256, 512), BF), half],
        both, *shards,
        in_specs=[VMEM] + [ANY] * 9,
        out_specs=[ANY, VMEM],
        scratch=[
            pltpu.VMEM((8, 256, 512), BF),
            pltpu.SemaphoreType.DMA((9,)),
            pltpu.SemaphoreType.DMA(()),
        ],
        flops=2 * 512 * 2048 * 512,
    )
    w_val, val, state = call(
        value_kernel,
        [((8, 16, 16, 512), BF), half, states],
        both, key, a, p1, p2, p3, b, r1, r2, r3,
        in_specs=[VMEM] * 2 + [ANY] * 8,
        out_specs=[ANY, VMEM, VMEM],
        scratch=[
            pltpu.VMEM((8, 16, 16, 512), BF),
            pltpu.SemaphoreType.DMA((32,)),
            pltpu.SemaphoreType.DMA(()),
        ],
        flops=2 * 512 * 2048 * 512,
    )

    def exchange(x, later, ahead):
        x = lax.all_to_all(x, "z", 0, 0, tiled=True)
        (x,) = call(
            lambda i, _, o: sums_kernel(later, i, o), [states], x, ahead, in_specs=[VMEM, ANY]
        )
        return lax.all_to_all(x, "z", 0, 0, tiled=True)

    qu, qf, scores, local = call(
        local_kernel,
        [half, half, ((8, 256, 256), BF), ((2 * rows, 512), F32)],
        queries, sib_q, key, val,
        flops=2 * 8 * 256 * 256 * 256,
    )
    before = exchange(state, False, local)
    out, grad_att, state = call(
        forward_kernel,
        [half, half, states],
        qf, out_grad, sib_g, local, before,
        flops=2 * 8 * 256 * 128 * 256,
    )
    dq, local_k, local_v = call(
        mixed_kernel,
        [half] + [((2 * rows, 512), F32)] * 2,
        qu, qf, key, val, scores, grad_att, before,
        flops=2 * 8 * 256 * 256 * 640,
    )
    after = exchange(state, True, local_v)
    sent = ((4, 128, 512), BF)
    dkv, a2, b2, a1, b1, a3, b3 = call(
        backward_kernel,
        [whole] + [sent] * 6,
        key, val, local_k, local_v, after, turned,
        in_specs=[VMEM] * 5 + [ANY],
        out_specs=[VMEM] + [ANY] * 6,
        scratch=[
            pltpu.VMEM((16, HD, 2 * rows), BF),
            pltpu.VMEM((6, 4, 128, 512), BF),
            pltpu.SemaphoreType.DMA(()),
            pltpu.SemaphoreType.DMA((6,)),
        ],
        flops=2 * 512 * 2048 * 1024,
    )
    wa, wb = {}, {}
    for d, to_x, to_y in ((2, a2, b2), (1, a1, b1), (3, a3, b3)):
        wa[d] = shift(to_x, "x", d)
        wb[d] = shift(to_y, "y", d)
    (back,) = call(pack_kernel, [((rows, 2048), BF)], dkv, dq, out, a2, in_specs=[VMEM] * 3 + [ANY])
    a0, b0 = call(
        own_kernel, [sent] * 2, turned, dkv, back, in_specs=[VMEM] * 2 + [ANY],
        flops=2 * 512 * 512 * 1024,
    )
    token_grad, output, query_grad = token_call(
        rows, dkv, swap(back), out, dq, w_key, swap(w_key), w_val, swap(w_val)
    )
    full = ((128, 512), F32)
    sent = ((128, 512), BF)
    parts = call(
        plane_kernel,
        [full, sent, sent, sent, full, sent, sent, sent],
        a0, wa[1], wa[2], wa[3], b0, wb[1], wb[2], wb[3], token_grad,
        in_specs=[ANY] * 9,
        scratch=[pltpu.VMEM((32, 128, 512), BF), pltpu.SemaphoreType.DMA((32,))],
    )
    wa, wb = {}, {}
    for d in (2, 1, 3):
        wa[d], wb[d] = shift(parts[d], "y", d), shift(parts[4 + d], "x", d)
    (column,) = call(
        column_kernel,
        [((16, 8, 1024), BF)],
        parts[0], wa[1], wa[2], wa[3], parts[4], wb[1], wb[2], wb[3],
    )
    column = lax.all_to_all(column, ("core", "z"), 0, 0, tiled=True)
    scale = 1.0 / math.sqrt(rows * lax.axis_size(("y", "x", "core", "z")))
    (weight_grad,) = call(lambda i, o: last_kernel(scale, i, o), [((8, 2048), F32)], column)
    return (output, token_grad, query_grad, weight_grad)


def solution(mesh):
    fine = Mesh(mesh.devices.reshape(4, 4, 2, 8), ("y", "x", "core", "z"))
    rows = P(("y", "x", "core", "z"), None)
    return jax.shard_map(
        on_device,
        mesh=fine,
        in_specs=(rows, rows, P("z", None), rows),
        out_specs=(rows, rows, rows, rows),
        check_vma=False,
    )
```

```python
import math

import jax
import jax.numpy as jnp
from jax import lax
from jax.experimental import pallas as pl
from jax.experimental.pallas import tpu as pltpu
from jax.sharding import Mesh
from jax.sharding import PartitionSpec as P


HD = 128
EPSILON = 1e-05
BF = jnp.bfloat16
F32 = jnp.float32
VMEM = pl.BlockSpec(memory_space=pltpu.VMEM)
ANY = pl.BlockSpec(memory_space=pl.ANY)


def feature(u):
    return jnp.where(u > 0, u + 1.0, jnp.exp(jnp.minimum(u, 0.0)))


def slope(u):
    return jnp.where(u > 0, 1.0, jnp.exp(jnp.minimum(u, 0.0)))


def dot(a, b, da, db):
    return lax.dot_general(a, b, (((da,), (db,)), ((), ())), preferred_element_type=F32)


def call(body, outs, *args, in_specs=None, out_specs=None, scratch=(), flops=0):
    size = sum(math.prod(a.shape) * a.dtype.itemsize for a in args)
    size += sum(math.prod(s) * jnp.dtype(d).itemsize for s, d in outs)
    return pl.pallas_call(
        body,
        out_shape=[jax.ShapeDtypeStruct(s, d) for s, d in outs],
        in_specs=in_specs or [VMEM] * len(args),
        out_specs=out_specs or [VMEM] * len(outs),
        scratch_shapes=list(scratch),
        cost_estimate=pl.CostEstimate(flops=flops, bytes_accessed=size, transcendentals=0),
    )(*args)


def shift(x, axis, step):
    size = lax.axis_size(axis)
    return lax.ppermute(x, axis, [(i, (i + step) % size) for i in range(size)])


def turn_kernel(own, sib, both, turned):
    both[:256] = own[...]
    both[256:] = sib[...]

    def step(n, _):
        at = pl.ds(pl.multiple_of(n * HD, HD), HD)
        turned[n, :, :256] = own[:, at].T
        turned[n, :, 256:] = sib[:, at].T
        return 0

    lax.fori_loop(0, 16, step, 0)


def project(tok, w_ref, out):
    def tile(n, _):
        at = pl.ds(pl.multiple_of(n * 256, 256), 256)
        if len(w_ref.shape) == 4:
            w = w_ref[:, :, :, at].reshape(2048, 256)
        else:
            w = w_ref[:, :, at].reshape(2048, 256)
        out[:, at] = dot(tok[...], w, 1, 0).astype(BF)
        return 0

    lax.fori_loop(0, 2, tile, 0)


def key_kernel(tok, *refs):
    shards, (w_out, key, w_ref, sems, out_sem) = refs[:8], refs[8:]
    z = lax.axis_index("z")
    copies = []
    for n, step in enumerate((0, -1, 1, -2, 2, -3, 3, 4)):
        to = w_ref.at[lax.rem(z + step + 8, 8)]
        copies.append(pltpu.make_async_copy(shards[n], to, sems.at[n]))
    for c in copies:
        c.start()
    for c in copies:
        c.wait()
    store = pltpu.make_async_copy(w_ref, w_out, out_sem)
    store.start()
    project(tok, w_ref, key)
    store.wait()


def value_kernel(tok, key, *refs):
    pieces, (w_out, val, state, w_ref, sems, out_sem) = refs[:8], refs[8:]
    y, x = lax.axis_index("y"), lax.axis_index("x")
    copies = []
    for half in range(2):
        for e in range(4):
            for d in range(4):
                py, px = (y - e, x - d) if half == 0 else (y - d, x - e)
                place = lax.rem(py + 4, 4) * 4 + lax.rem(px + 4, 4)
                copies.append(
                    pltpu.make_async_copy(
                        pieces[half * 4 + e].at[d],
                        w_ref.at[:, place, :, pl.ds(half * 256, 256)],
                        sems.at[len(copies)],
                    )
                )
    for c in copies:
        c.start()
    for c in copies:
        c.wait()
    project(tok, w_ref, val)
    store = pltpu.make_async_copy(w_ref, w_out, out_sem)
    store.start()

    def body(n, rows, at):
        k = feature(key[rows, at].astype(F32)).astype(BF)
        state[n] = dot(k, val[rows, at], 0, 0).astype(BF)

    each_spot(body)
    store.wait()


def sums_kernel(later, states, out):
    order = list(range(states.shape[0]))
    if later:
        order.reverse()
    total = jnp.zeros(states.shape[1:], F32)
    for k in order:
        out[k] = total.astype(BF)
        total = total + states[k].astype(F32)


def causal():
    shape = (256, 256)
    return lax.broadcasted_iota(jnp.int32, shape, 0) >= lax.broadcasted_iota(jnp.int32, shape, 1)


def each_spot(body):
    def step(h, _):
        for s in range(2):
            at = pl.ds(pl.multiple_of(h * HD, HD), HD)
            body(s * 4 + h, slice(s * 256, s * 256 + 256), at)
        return 0

    lax.fori_loop(0, 4, step, 0)


def local_kernel(q_own, q_sib, key, val, qu, qf, scores, local):
    mask = causal()
    at = lax.axis_index("core") * 512
    qu[:256] = q_own[:, pl.ds(pl.multiple_of(at, 512), 512)]
    qu[256:] = q_sib[...]

    def body(n, rows, at):
        q = feature(qu[rows, at].astype(F32)).astype(BF)
        qf[rows, at] = q
        k = feature(key[rows, at].astype(F32)).astype(BF)
        score = jnp.where(mask, dot(q, k, 1, 1), 0.0).astype(BF)
        scores[n] = score
        local[rows, at] = dot(score, val[rows, at], 1, 0)

    each_spot(body)


def forward_kernel(qf, g_own, g_sib, local, before, out, grad_att, state):
    core = lax.axis_index("core")

    def step(h, _):
        at = pl.ds(pl.multiple_of(h * HD, HD), HD)
        mine = pl.ds(pl.multiple_of(core * 512 + h * HD, HD), HD)
        for s, (g_ref, g_at) in enumerate(((g_own, mine), (g_sib, at))):
            n, rows = s * 4 + h, slice(s * 256, s * 256 + 256)
            q, g = qf[rows, at], g_ref[:, g_at].astype(F32)
            attended = local[rows, at] + dot(q, before[n], 1, 0)
            power = jnp.mean(attended * attended, axis=-1, keepdims=True) + EPSILON
            inverse = lax.rsqrt(power)
            normed = attended * inverse
            along = jnp.mean(g * normed, axis=-1, keepdims=True)
            grad = ((g - normed * along) * inverse).astype(BF)
            out[rows, at] = normed.astype(BF)
            grad_att[rows, at] = grad
            state[n] = dot(q, grad, 0, 0).astype(BF)
        return 0

    lax.fori_loop(0, 4, step, 0)


def mixed_kernel(qu, qf, key, val, scores, grad_att, before, dq, local_k, local_v):
    mask = causal()

    def body(n, rows, at):
        u, q = qu[rows, at].astype(F32), qf[rows, at]
        k = feature(key[rows, at].astype(F32)).astype(BF)
        a = grad_att[rows, at]
        mixed = jnp.where(mask, dot(a, val[rows, at], 1, 1), 0.0).astype(BF)
        grad_q = dot(mixed, k, 1, 0) + dot(a, before[n], 1, 1)
        dq[rows, at] = (grad_q * slope(u)).astype(BF)
        local_k[rows, at] = dot(mixed, q, 0, 0)
        local_v[rows, at] = dot(scores[n], a, 0, 0)

    each_spot(body)


def chunk(half, d, turned, dkv):
    if half == 0:
        to = lax.rem(lax.axis_index("x") + d, 4)
        tok = jnp.concatenate([turned[n * 4 + to] for n in range(4)], axis=0)
    else:
        to = lax.rem(lax.axis_index("y") + d, 4)
        tok = turned[pl.ds(to * 4, 4)].reshape(512, 512)
    part = dot(tok, dkv[:, half * 512 : half * 512 + 512], 1, 0)
    return part.astype(BF).reshape(4, 128, 512)


STEPS = (2, 1, 3)


def backward_kernel(key, val, local_k, local_v, after, turned_hbm, dkv, *refs):
    outs, (turned, held, sem, sems) = refs[:6], refs[6:]
    load = pltpu.make_async_copy(turned_hbm, turned, sem)
    load.start()

    def body(n, rows, at):
        u = key[rows, at].astype(F32)
        k, v = feature(u).astype(BF), val[rows, at]
        vat = pl.ds(pl.multiple_of(512 + at.start, HD), HD)
        grad_k = local_k[rows, at] + dot(v, after[n], 1, 1)
        grad_v = local_v[rows, at] + dot(k, after[n], 1, 0)
        dkv[rows, at] = (grad_k * slope(u)).astype(BF)
        dkv[rows, vat] = grad_v.astype(BF)

    each_spot(body)
    load.wait()
    stores = []
    for i, d in enumerate(STEPS):
        for half in range(2):
            n = 2 * i + half
            held[n] = chunk(half, d, turned, dkv)
            stores.append(pltpu.make_async_copy(held.at[n], outs[n], sems.at[n]))
            stores[-1].start()
    for c in stores:
        c.wait()


def own_kernel(turned, dkv, _, a_ref, b_ref):
    y, x = lax.axis_index("y"), lax.axis_index("x")

    def step(n, _):
        for to, chip, half in ((a_ref, n * 4 + x, 0), (b_ref, y * 4 + n, 1)):
            part = dot(turned[chip], dkv[:, half * 512 : half * 512 + 512], 1, 0)
            to[n] = part.astype(BF)
        return 0

    lax.fori_loop(0, 4, step, 0)


def pack_kernel(dkv, dq, out, _, back):
    back[:, :1024] = dkv[256:]
    back[:, 1024:1536] = dq[256:]
    back[:, 1536:] = out[256:]


def plane_kernel(*refs):
    ins, outs, (held, sems) = refs[:8], refs[9:17], refs[17:]
    y, x = lax.axis_index("y"), lax.axis_index("x")
    loads = {}
    for e in (2, 1, 3, 0):
        for half, here in ((0, y), (1, x)):
            at = lax.rem(here + e, 4)
            for k in range(4):
                n = (e * 2 + half) * 4 + k
                loads[n] = pltpu.make_async_copy(ins[half * 4 + k].at[at], held.at[n], sems.at[n])
                loads[n].start()
    for e in (2, 1, 3, 0):
        for half in range(2):
            first = (e * 2 + half) * 4
            for n in range(first, first + 4):
                loads[n].wait()
            total = held[first].astype(F32)
            for n in range(first + 1, first + 4):
                total = total + held[n].astype(F32)
            to = outs[half * 4 + e]
            to[...] = total.astype(to.dtype)


def column_kernel(*refs):
    out = refs[-1]

    def step(n, _):
        rows = pl.ds(pl.multiple_of(n * 64, 64), 64)
        for half in range(2):
            total = refs[half * 4][rows]
            for r in refs[half * 4 + 1 : half * 4 + 4]:
                total = total + r[rows].astype(F32)
            at = slice(half * 512, half * 512 + 512)
            out[pl.ds(n * 8, 8), :, at] = total.reshape(8, 8, 512).astype(BF)
        return 0

    lax.fori_loop(0, 2, step, 0)


def last_kernel(scale, parts, out):
    for c in range(2):
        total = parts[c * 8].astype(F32)
        for k in range(1, 8):
            total = total + parts[c * 8 + k].astype(F32)
        total = total * scale
        for half in range(2):
            at = half * 1024 + c * 512
            out[:, at : at + 512] = total[:, half * 512 : half * 512 + 512]


def token_kernel(dkv, got, o, dq, wk, wk_sib, wv, wv_sib, out, o_out, dq_out):
    total = dot(dkv[:256, :512], wk[0], 1, 1) + dot(got[:, :512], wk_sib[0], 1, 1)
    total += dot(dkv[:256, 512:], wv[0].reshape(256, 512), 1, 1)
    total += dot(got[:, 512:1024], wv_sib[0].reshape(256, 512), 1, 1)
    out[...] = total.astype(BF)

    @pl.when(pl.program_id(0) == 0)
    def _():
        core = lax.axis_index("core")
        mine = pl.ds(pl.multiple_of(core * 512, 512), 512)
        other = pl.ds(pl.multiple_of((1 - core) * 512, 512), 512)
        o_out[:, mine] = o[:256]
        o_out[:, other] = got[:, 1536:]
        dq_out[:, mine] = dq[:256]
        dq_out[:, other] = got[:, 1024:1536]


def token_call(rows, *args):
    def fixed(shape):
        return pl.BlockSpec(shape, lambda n: (0,) * len(shape))

    tile_k = pl.BlockSpec((1, 256, 512), lambda n: (n, 0, 0))
    tile_v = pl.BlockSpec((1, 16, 16, 512), lambda n: (n, 0, 0, 0))
    return pl.pallas_call(
        token_kernel,
        grid=(8,),
        out_shape=[jax.ShapeDtypeStruct((rows, n), BF) for n in (2048, 1024, 1024)],
        in_specs=[fixed(a.shape) for a in args[:4]] + [tile_k] * 2 + [tile_v] * 2,
        out_specs=[pl.BlockSpec((rows, 256), lambda n: (0, n))] + [fixed((rows, 1024))] * 2,
        cost_estimate=pl.CostEstimate(
            flops=4 * 2 * rows * 2048 * 2048, bytes_accessed=12 << 20, transcendentals=0
        ),
    )(*args)


def on_device(tokens, queries, kv_weight, out_grad):
    rows = tokens.shape[0]
    core = lax.axis_index("core")

    def swap(x):
        return lax.ppermute(x, "core", [(0, 1), (1, 0)])

    def theirs(x):
        return swap(lax.dynamic_slice_in_dim(x, (1 - core) * 512, 512, 1))

    shard = lax.dynamic_slice_in_dim(kv_weight, core * 512, 512, 1)
    shards, left, right = [shard], shard, shard
    for _ in range(3):
        left, right = shift(left, "z", 1), shift(right, "z", -1)
        shards += [left, right]
    shards.append(shift(left, "z", 1))
    place = lax.axis_index(("y", "x"))
    mine = lax.dynamic_slice(kv_weight, (place * 16, 1024 + core * 512), (16, 512))
    mine = jnp.broadcast_to(mine[None], (8, 16, 512))
    along_z = lax.all_to_all(mine, "z", 0, 0, tiled=True)
    a0, b0 = along_z[:, :, :256], along_z[:, :, 256:]
    (a2, b2), (a1, b1), (a3, b3) = [(shift(a0, "x", d), shift(b0, "y", d)) for d in (2, 1, 3)]
    a = jnp.stack([a0, a1, a2, a3])
    b = jnp.stack([b0, b1, b2, b3])
    (p2, r2), (p1, r1), (p3, r3) = [(shift(a, "y", e), shift(b, "x", e)) for e in (2, 1, 3)]

    sib_tokens = swap(tokens)
    sib_q, sib_g = theirs(queries), theirs(out_grad)
    both, turned = call(
        turn_kernel,
        [((2 * rows, 2048), BF), ((16, HD, 2 * rows), BF)],
        tokens, sib_tokens,
    )
    half = ((2 * rows, 512), BF)
    whole = ((2 * rows, 1024), BF)
    states = ((8, HD, HD), BF)
    w_key, key = call(
        key_kernel,
        [((8, 256, 512), BF), half],
        both, *shards,
        in_specs=[VMEM] + [ANY] * 8,
        out_specs=[ANY, VMEM],
        scratch=[
            pltpu.VMEM((8, 256, 512), BF),
            pltpu.SemaphoreType.DMA((8,)),
            pltpu.SemaphoreType.DMA(()),
        ],
        flops=2 * 512 * 2048 * 512,
    )
    w_val, val, state = call(
        value_kernel,
        [((8, 16, 16, 512), BF), half, states],
        both, key, a, p1, p2, p3, b, r1, r2, r3,
        in_specs=[VMEM] * 2 + [ANY] * 8,
        out_specs=[ANY, VMEM, VMEM],
        scratch=[
            pltpu.VMEM((8, 16, 16, 512), BF),
            pltpu.SemaphoreType.DMA((32,)),
            pltpu.SemaphoreType.DMA(()),
        ],
        flops=2 * 512 * 2048 * 512,
    )

    def exchange(x, later, ahead):
        x = lax.all_to_all(x, "z", 0, 0, tiled=True)
        (x,) = call(
            lambda i, _, o: sums_kernel(later, i, o), [states], x, ahead, in_specs=[VMEM, ANY]
        )
        return lax.all_to_all(x, "z", 0, 0, tiled=True)

    qu, qf, scores, local = call(
        local_kernel,
        [half, half, ((8, 256, 256), BF), ((2 * rows, 512), F32)],
        queries, sib_q, key, val,
        flops=2 * 8 * 256 * 256 * 256,
    )
    before = exchange(state, False, local)
    out, grad_att, state = call(
        forward_kernel,
        [half, half, states],
        qf, out_grad, sib_g, local, before,
        flops=2 * 8 * 256 * 128 * 256,
    )
    dq, local_k, local_v = call(
        mixed_kernel,
        [half] + [((2 * rows, 512), F32)] * 2,
        qu, qf, key, val, scores, grad_att, before,
        flops=2 * 8 * 256 * 256 * 640,
    )
    after = exchange(state, True, local_v)
    sent = ((4, 128, 512), BF)
    dkv, a2, b2, a1, b1, a3, b3 = call(
        backward_kernel,
        [whole] + [sent] * 6,
        key, val, local_k, local_v, after, turned,
        in_specs=[VMEM] * 5 + [ANY],
        out_specs=[VMEM] + [ANY] * 6,
        scratch=[
            pltpu.VMEM((16, HD, 2 * rows), BF),
            pltpu.VMEM((6, 4, 128, 512), BF),
            pltpu.SemaphoreType.DMA(()),
            pltpu.SemaphoreType.DMA((6,)),
        ],
        flops=2 * 512 * 2048 * 1024,
    )
    wa, wb = {}, {}
    for d, to_x, to_y in ((2, a2, b2), (1, a1, b1), (3, a3, b3)):
        wa[d] = shift(to_x, "x", d)
        wb[d] = shift(to_y, "y", d)
    (back,) = call(pack_kernel, [((rows, 2048), BF)], dkv, dq, out, a2, in_specs=[VMEM] * 3 + [ANY])
    a0, b0 = call(
        own_kernel, [sent] * 2, turned, dkv, back, in_specs=[VMEM] * 2 + [ANY],
        flops=2 * 512 * 512 * 1024,
    )
    token_grad, output, query_grad = token_call(
        rows, dkv, swap(back), out, dq, w_key, swap(w_key), w_val, swap(w_val)
    )
    full = ((128, 512), F32)
    sent = ((128, 512), BF)
    parts = call(
        plane_kernel,
        [full, sent, sent, sent, full, sent, sent, sent],
        a0, wa[1], wa[2], wa[3], b0, wb[1], wb[2], wb[3], token_grad,
        in_specs=[ANY] * 9,
        scratch=[pltpu.VMEM((32, 128, 512), BF), pltpu.SemaphoreType.DMA((32,))],
    )
    wa, wb = {}, {}
    for d in (2, 1, 3):
        wa[d], wb[d] = shift(parts[d], "y", d), shift(parts[4 + d], "x", d)
    (column,) = call(
        column_kernel,
        [((16, 8, 1024), BF)],
        parts[0], wa[1], wa[2], wa[3], parts[4], wb[1], wb[2], wb[3],
    )
    column = lax.all_to_all(column, ("core", "z"), 0, 0, tiled=True)
    scale = 1.0 / math.sqrt(rows * lax.axis_size(("y", "x", "core", "z")))
    (weight_grad,) = call(lambda i, o: last_kernel(scale, i, o), [((8, 2048), F32)], column)
    return (output, token_grad, query_grad, weight_grad)


def solution(mesh):
    fine = Mesh(mesh.devices.reshape(4, 4, 2, 8), ("y", "x", "core", "z"))
    rows = P(("y", "x", "core", "z"), None)
    return jax.shard_map(
        on_device,
        mesh=fine,
        in_specs=(rows, rows, P("z", None), rows),
        out_specs=(rows, rows, rows, rows),
        check_vma=False,
    )
```

```python
import math

import jax
import jax.numpy as jnp
from jax import lax
from jax.experimental import pallas as pl
from jax.experimental.pallas import tpu as pltpu
from jax.sharding import Mesh
from jax.sharding import PartitionSpec as P


HD = 128
EPSILON = 1e-05
BF = jnp.bfloat16
F32 = jnp.float32
VMEM = pl.BlockSpec(memory_space=pltpu.VMEM)
ANY = pl.BlockSpec(memory_space=pl.ANY)


def feature(u):
    return jnp.where(u > 0, u + 1.0, jnp.exp(jnp.minimum(u, 0.0)))


def slope(u):
    return jnp.where(u > 0, 1.0, jnp.exp(jnp.minimum(u, 0.0)))


def dot(a, b, da, db):
    return lax.dot_general(a, b, (((da,), (db,)), ((), ())), preferred_element_type=F32)


def call(body, outs, *args, in_specs=None, out_specs=None, scratch=(), flops=0):
    size = sum(math.prod(a.shape) * a.dtype.itemsize for a in args)
    size += sum(math.prod(s) * jnp.dtype(d).itemsize for s, d in outs)
    return pl.pallas_call(
        body,
        out_shape=[jax.ShapeDtypeStruct(s, d) for s, d in outs],
        in_specs=in_specs or [VMEM] * len(args),
        out_specs=out_specs or [VMEM] * len(outs),
        scratch_shapes=list(scratch),
        cost_estimate=pl.CostEstimate(flops=flops, bytes_accessed=size, transcendentals=0),
    )(*args)


def shift(x, axis, step):
    size = lax.axis_size(axis)
    return lax.ppermute(x, axis, [(i, (i + step) % size) for i in range(size)])


def turn_kernel(own, sib, both, turned):
    both[:256] = own[...]
    both[256:] = sib[...]

    def step(n, _):
        at = pl.ds(pl.multiple_of(n * HD, HD), HD)
        turned[n, :, :256] = own[:, at].T
        turned[n, :, 256:] = sib[:, at].T
        return 0

    lax.fori_loop(0, 16, step, 0)


def project(tok, w_ref, out):
    def tile(n, _):
        at = pl.ds(pl.multiple_of(n * 256, 256), 256)
        if len(w_ref.shape) == 4:
            w = w_ref[:, :, :, at].reshape(2048, 256)
        else:
            w = w_ref[:, :, at].reshape(2048, 256)
        out[:, at] = dot(tok[...], w, 1, 0).astype(BF)
        return 0

    lax.fori_loop(0, 2, tile, 0)


def key_kernel(tok, *refs):
    shards, (w_out, key, w_ref, sems, out_sem) = refs[:8], refs[8:]
    z = lax.axis_index("z")
    copies = []
    for n, step in enumerate((0, -1, 1, -2, 2, -3, 3, 4)):
        to = w_ref.at[lax.rem(z + step + 8, 8)]
        copies.append(pltpu.make_async_copy(shards[n], to, sems.at[n]))
    for c in copies:
        c.start()
    for c in copies:
        c.wait()
    store = pltpu.make_async_copy(w_ref, w_out, out_sem)
    store.start()
    project(tok, w_ref, key)
    store.wait()


def value_kernel(tok, key, *refs):
    pieces, (w_out, val, state, w_ref, sems, out_sem) = refs[:8], refs[8:]
    y, x = lax.axis_index("y"), lax.axis_index("x")
    copies = []
    for half in range(2):
        for e in range(4):
            for d in range(4):
                py, px = (y - e, x - d) if half == 0 else (y - d, x - e)
                place = lax.rem(py + 4, 4) * 4 + lax.rem(px + 4, 4)
                copies.append(
                    pltpu.make_async_copy(
                        pieces[half * 4 + e].at[d],
                        w_ref.at[:, place, :, pl.ds(half * 256, 256)],
                        sems.at[len(copies)],
                    )
                )
    for c in copies:
        c.start()
    for c in copies:
        c.wait()
    project(tok, w_ref, val)
    store = pltpu.make_async_copy(w_ref, w_out, out_sem)
    store.start()

    def body(n, rows, at):
        k = feature(key[rows, at].astype(F32)).astype(BF)
        state[n] = dot(k, val[rows, at], 0, 0).astype(BF)

    each_spot(body)
    store.wait()


def sums_kernel(later, states, out):
    order = list(range(states.shape[0]))
    if later:
        order.reverse()
    total = jnp.zeros(states.shape[1:], F32)
    for k in order:
        out[k] = total.astype(BF)
        total = total + states[k].astype(F32)


def causal():
    shape = (256, 256)
    return lax.broadcasted_iota(jnp.int32, shape, 0) >= lax.broadcasted_iota(jnp.int32, shape, 1)


def each_spot(body):
    def step(h, _):
        for s in range(2):
            at = pl.ds(pl.multiple_of(h * HD, HD), HD)
            body(s * 4 + h, slice(s * 256, s * 256 + 256), at)
        return 0

    lax.fori_loop(0, 4, step, 0)


def local_kernel(q_own, q_sib, key, val, qu, qf, scores, local):
    mask = causal()
    at = lax.axis_index("core") * 512
    qu[:256] = q_own[:, pl.ds(pl.multiple_of(at, 512), 512)]
    qu[256:] = q_sib[...]

    def body(n, rows, at):
        q = feature(qu[rows, at].astype(F32)).astype(BF)
        qf[rows, at] = q
        k = feature(key[rows, at].astype(F32)).astype(BF)
        score = jnp.where(mask, dot(q, k, 1, 1), 0.0).astype(BF)
        scores[n] = score
        local[rows, at] = dot(score, val[rows, at], 1, 0)

    each_spot(body)


def forward_kernel(qf, g_own, g_sib, local, before, out, grad_att, state):
    core = lax.axis_index("core")

    def step(h, _):
        at = pl.ds(pl.multiple_of(h * HD, HD), HD)
        mine = pl.ds(pl.multiple_of(core * 512 + h * HD, HD), HD)
        for s, (g_ref, g_at) in enumerate(((g_own, mine), (g_sib, at))):
            n, rows = s * 4 + h, slice(s * 256, s * 256 + 256)
            q, g = qf[rows, at], g_ref[:, g_at].astype(F32)
            attended = local[rows, at] + dot(q, before[n], 1, 0)
            power = jnp.mean(attended * attended, axis=-1, keepdims=True) + EPSILON
            inverse = lax.rsqrt(power)
            normed = attended * inverse
            along = jnp.mean(g * normed, axis=-1, keepdims=True)
            grad = ((g - normed * along) * inverse).astype(BF)
            out[rows, at] = normed.astype(BF)
            grad_att[rows, at] = grad
            state[n] = dot(q, grad, 0, 0).astype(BF)
        return 0

    lax.fori_loop(0, 4, step, 0)


def mixed_kernel(qu, qf, key, val, scores, grad_att, before, dq, local_k, local_v):
    mask = causal()

    def body(n, rows, at):
        u, q = qu[rows, at].astype(F32), qf[rows, at]
        k = feature(key[rows, at].astype(F32)).astype(BF)
        a = grad_att[rows, at]
        mixed = jnp.where(mask, dot(a, val[rows, at], 1, 1), 0.0).astype(BF)
        grad_q = dot(mixed, k, 1, 0) + dot(a, before[n], 1, 1)
        dq[rows, at] = (grad_q * slope(u)).astype(BF)
        local_k[rows, at] = dot(mixed, q, 0, 0)
        local_v[rows, at] = dot(scores[n], a, 0, 0)

    each_spot(body)


def chunk(half, d, turned, dkv):
    if half == 0:
        to = lax.rem(lax.axis_index("x") + d, 4)
        tok = jnp.concatenate([turned[n * 4 + to] for n in range(4)], axis=0)
    else:
        to = lax.rem(lax.axis_index("y") + d, 4)
        tok = turned[pl.ds(to * 4, 4)].reshape(512, 512)
    part = dot(tok, dkv[:, half * 512 : half * 512 + 512], 1, 0)
    return part.astype(BF).reshape(4, 128, 512)


STEPS = (2, 1, 3)


def backward_kernel(key, val, local_k, local_v, after, turned_hbm, dkv, *refs):
    outs, (turned, held, sem, sems) = refs[:6], refs[6:]
    load = pltpu.make_async_copy(turned_hbm, turned, sem)
    load.start()

    def body(n, rows, at):
        u = key[rows, at].astype(F32)
        k, v = feature(u).astype(BF), val[rows, at]
        vat = pl.ds(pl.multiple_of(512 + at.start, HD), HD)
        grad_k = local_k[rows, at] + dot(v, after[n], 1, 1)
        grad_v = local_v[rows, at] + dot(k, after[n], 1, 0)
        dkv[rows, at] = (grad_k * slope(u)).astype(BF)
        dkv[rows, vat] = grad_v.astype(BF)

    each_spot(body)
    load.wait()
    stores = []
    for i, d in enumerate(STEPS):
        for half in range(2):
            n = 2 * i + half
            held[n] = chunk(half, d, turned, dkv)
            stores.append(pltpu.make_async_copy(held.at[n], outs[n], sems.at[n]))
            stores[-1].start()
    for c in stores:
        c.wait()


def own_kernel(turned, dkv, _, a_ref, b_ref):
    y, x = lax.axis_index("y"), lax.axis_index("x")

    def step(n, _):
        for to, chip, half in ((a_ref, n * 4 + x, 0), (b_ref, y * 4 + n, 1)):
            part = dot(turned[chip], dkv[:, half * 512 : half * 512 + 512], 1, 0)
            to[n] = part.astype(BF)
        return 0

    lax.fori_loop(0, 4, step, 0)


def pack_kernel(dkv, dq, out, _, back):
    back[:, :1024] = dkv[256:]
    back[:, 1024:1536] = dq[256:]
    back[:, 1536:] = out[256:]


def plane_kernel(*refs):
    ins, outs, (held, sems) = refs[:8], refs[9:17], refs[17:]
    y, x = lax.axis_index("y"), lax.axis_index("x")
    loads = {}
    for e in (2, 1, 3, 0):
        for half, here in ((0, y), (1, x)):
            at = lax.rem(here + e, 4)
            for k in range(4):
                n = (e * 2 + half) * 4 + k
                loads[n] = pltpu.make_async_copy(ins[half * 4 + k].at[at], held.at[n], sems.at[n])
                loads[n].start()
    for e in (2, 1, 3, 0):
        for half in range(2):
            first = (e * 2 + half) * 4
            for n in range(first, first + 4):
                loads[n].wait()
            total = held[first].astype(F32)
            for n in range(first + 1, first + 4):
                total = total + held[n].astype(F32)
            to = outs[half * 4 + e]
            to[...] = total.astype(to.dtype)


def column_kernel(*refs):
    out = refs[-1]

    def step(n, _):
        rows = pl.ds(pl.multiple_of(n * 64, 64), 64)
        for half in range(2):
            total = refs[half * 4][rows]
            for r in refs[half * 4 + 1 : half * 4 + 4]:
                total = total + r[rows].astype(F32)
            at = slice(half * 512, half * 512 + 512)
            out[pl.ds(n * 8, 8), :, at] = total.reshape(8, 8, 512).astype(BF)
        return 0

    lax.fori_loop(0, 2, step, 0)


def last_kernel(scale, parts, out):
    for c in range(2):
        total = parts[c * 8].astype(F32)
        for k in range(1, 8):
            total = total + parts[c * 8 + k].astype(F32)
        total = total * scale
        for half in range(2):
            at = half * 1024 + c * 512
            out[:, at : at + 512] = total[:, half * 512 : half * 512 + 512]


def token_kernel(dkv, got, o, dq, wk, wk_sib, wv, wv_sib, out, o_out, dq_out):
    total = dot(dkv[:256, :512], wk[0], 1, 1) + dot(got[:, :512], wk_sib[0], 1, 1)
    total += dot(dkv[:256, 512:], wv[0].reshape(256, 512), 1, 1)
    total += dot(got[:, 512:1024], wv_sib[0].reshape(256, 512), 1, 1)
    out[...] = total.astype(BF)

    @pl.when(pl.program_id(0) == 0)
    def _():
        core = lax.axis_index("core")
        mine = pl.ds(pl.multiple_of(core * 512, 512), 512)
        other = pl.ds(pl.multiple_of((1 - core) * 512, 512), 512)
        o_out[:, mine] = o[:256]
        o_out[:, other] = got[:, 1536:]
        dq_out[:, mine] = dq[:256]
        dq_out[:, other] = got[:, 1024:1536]


def token_call(rows, *args):
    def fixed(shape):
        return pl.BlockSpec(shape, lambda n: (0,) * len(shape))

    tile_k = pl.BlockSpec((1, 256, 512), lambda n: (n, 0, 0))
    tile_v = pl.BlockSpec((1, 16, 16, 512), lambda n: (n, 0, 0, 0))
    return pl.pallas_call(
        token_kernel,
        grid=(8,),
        out_shape=[jax.ShapeDtypeStruct((rows, n), BF) for n in (2048, 1024, 1024)],
        in_specs=[fixed(a.shape) for a in args[:4]] + [tile_k] * 2 + [tile_v] * 2,
        out_specs=[pl.BlockSpec((rows, 256), lambda n: (0, n))] + [fixed((rows, 1024))] * 2,
        cost_estimate=pl.CostEstimate(
            flops=4 * 2 * rows * 2048 * 2048, bytes_accessed=12 << 20, transcendentals=0
        ),
    )(*args)


def on_device(tokens, queries, kv_weight, out_grad):
    rows = tokens.shape[0]
    core = lax.axis_index("core")

    def swap(x):
        return lax.ppermute(x, "core", [(0, 1), (1, 0)])

    def theirs(x):
        return swap(lax.dynamic_slice_in_dim(x, (1 - core) * 512, 512, 1))

    shard = lax.dynamic_slice_in_dim(kv_weight, core * 512, 512, 1)
    shards, left, right = [shard], shard, shard
    for _ in range(3):
        left = shift(left, "z", 1)
        right = shift(right, "z", -1)
        shards += [left, right]
    shards.append(shift(left, "z", 1))
    place = lax.axis_index(("y", "x"))
    mine = lax.dynamic_slice(kv_weight, (place * 16, 1024 + core * 512), (16, 512))
    mine = jnp.broadcast_to(mine[None], (8, 16, 512))
    along_z = lax.all_to_all(mine, "z", 0, 0, tiled=True)
    a0, b0 = along_z[:, :, :256], along_z[:, :, 256:]
    got_a, got_b = {}, {}
    for d in STEPS:
        got_a[d] = shift(a0, "x", d)
        got_b[d] = shift(b0, "y", d)
    (a1, a2, a3), (b1, b2, b3) = ([got[d] for d in (1, 2, 3)] for got in (got_a, got_b))
    a = jnp.stack([a0, a1, a2, a3])
    b = jnp.stack([b0, b1, b2, b3])
    (p2, r2), (p1, r1), (p3, r3) = [(shift(a, "y", e), shift(b, "x", e)) for e in (2, 1, 3)]

    sib_tokens = swap(tokens)
    sib_q, sib_g = theirs(queries), theirs(out_grad)
    both, turned = call(
        turn_kernel,
        [((2 * rows, 2048), BF), ((16, HD, 2 * rows), BF)],
        tokens, sib_tokens,
    )
    half = ((2 * rows, 512), BF)
    whole = ((2 * rows, 1024), BF)
    states = ((8, HD, HD), BF)
    w_key, key = call(
        key_kernel,
        [((8, 256, 512), BF), half],
        both, *shards,
        in_specs=[VMEM] + [ANY] * 8,
        out_specs=[ANY, VMEM],
        scratch=[
            pltpu.VMEM((8, 256, 512), BF),
            pltpu.SemaphoreType.DMA((8,)),
            pltpu.SemaphoreType.DMA(()),
        ],
        flops=2 * 512 * 2048 * 512,
    )
    w_val, val, state = call(
        value_kernel,
        [((8, 16, 16, 512), BF), half, states],
        both, key, a, p1, p2, p3, b, r1, r2, r3,
        in_specs=[VMEM] * 2 + [ANY] * 8,
        out_specs=[ANY, VMEM, VMEM],
        scratch=[
            pltpu.VMEM((8, 16, 16, 512), BF),
            pltpu.SemaphoreType.DMA((32,)),
            pltpu.SemaphoreType.DMA(()),
        ],
        flops=2 * 512 * 2048 * 512,
    )

    def exchange(x, later, ahead):
        x = lax.all_to_all(x, "z", 0, 0, tiled=True)
        (x,) = call(
            lambda i, _, o: sums_kernel(later, i, o), [states], x, ahead, in_specs=[VMEM, ANY]
        )
        return lax.all_to_all(x, "z", 0, 0, tiled=True)

    qu, qf, scores, local = call(
        local_kernel,
        [half, half, ((8, 256, 256), BF), ((2 * rows, 512), F32)],
        queries, sib_q, key, val,
        flops=2 * 8 * 256 * 256 * 256,
    )
    before = exchange(state, False, local)
    out, grad_att, state = call(
        forward_kernel,
        [half, half, states],
        qf, out_grad, sib_g, local, before,
        flops=2 * 8 * 256 * 128 * 256,
    )
    dq, local_k, local_v = call(
        mixed_kernel,
        [half] + [((2 * rows, 512), F32)] * 2,
        qu, qf, key, val, scores, grad_att, before,
        flops=2 * 8 * 256 * 256 * 640,
    )
    after = exchange(state, True, local_v)
    sent = ((4, 128, 512), BF)
    dkv, a2, b2, a1, b1, a3, b3 = call(
        backward_kernel,
        [whole] + [sent] * 6,
        key, val, local_k, local_v, after, turned,
        in_specs=[VMEM] * 5 + [ANY],
        out_specs=[VMEM] + [ANY] * 6,
        scratch=[
            pltpu.VMEM((16, HD, 2 * rows), BF),
            pltpu.VMEM((6, 4, 128, 512), BF),
            pltpu.SemaphoreType.DMA(()),
            pltpu.SemaphoreType.DMA((6,)),
        ],
        flops=2 * 512 * 2048 * 1024,
    )
    wa, wb = {}, {}
    for d, to_x, to_y in ((2, a2, b2), (1, a1, b1), (3, a3, b3)):
        wa[d] = shift(to_x, "x", d)
        wb[d] = shift(to_y, "y", d)
    (back,) = call(
        pack_kernel, [((rows, 2048), BF)], dkv, dq, out, a2, in_specs=[VMEM] * 3 + [ANY]
    )
    a0, b0 = call(
        own_kernel, [sent] * 2, turned, dkv, back, in_specs=[VMEM] * 2 + [ANY],
        flops=2 * 512 * 512 * 1024,
    )
    token_grad, output, query_grad = token_call(
        rows, dkv, swap(back), out, dq, w_key, swap(w_key), w_val, swap(w_val)
    )
    full = ((128, 512), F32)
    sent = ((128, 512), BF)
    parts = call(
        plane_kernel,
        [full, sent, sent, sent, full, sent, sent, sent],
        a0, wa[1], wa[2], wa[3], b0, wb[1], wb[2], wb[3], token_grad,
        in_specs=[ANY] * 9,
        scratch=[pltpu.VMEM((32, 128, 512), BF), pltpu.SemaphoreType.DMA((32,))],
    )
    wa, wb = {}, {}
    for d in (2, 1, 3):
        wa[d], wb[d] = shift(parts[d], "y", d), shift(parts[4 + d], "x", d)
    (column,) = call(
        column_kernel,
        [((16, 8, 1024), BF)],
        parts[0], wa[1], wa[2], wa[3], parts[4], wb[1], wb[2], wb[3],
    )
    column = lax.all_to_all(column, ("core", "z"), 0, 0, tiled=True)
    scale = 1.0 / math.sqrt(rows * lax.axis_size(("y", "x", "core", "z")))
    (weight_grad,) = call(lambda i, o: last_kernel(scale, i, o), [((8, 2048), F32)], column)
    return (output, token_grad, query_grad, weight_grad)


def solution(mesh):
    fine = Mesh(mesh.devices.reshape(4, 4, 2, 8), ("y", "x", "core", "z"))
    rows = P(("y", "x", "core", "z"), None)
    return jax.shard_map(
        on_device,
        mesh=fine,
        in_specs=(rows, rows, P("z", None), rows),
        out_specs=(rows, rows, rows, rows),
        check_vma=False,
    )
```
